256 devices in a mesh: row: 16 (over z_hi, x), col: 16 (over z_lo, y, core).
Axes of the slice: x: 4, y: 4, z: 8 (z_hi: 4, z_lo: 2; z = z_hi * 2 + z_lo), core: 2. Of those that a mesh axis runs over, the one named last changes fastest.
Arguments:
- signal: bfloat16 [32768, 2048], P('row', 'col'), may hold values from -40 to 40
- norm_gain: float32 [2048], replicated, may hold values from 0.5 to 2
- qkv_weight: bfloat16 [2048, 6144], P('row', 'col'), may hold values from -4 to 4
- out_weight: bfloat16 [2048, 2048], P('row', 'col'), may hold values from -1 to 1
Outputs:
- layer_out: bfloat16 [32768, 2048], P('row', 'col')
The draws below stay inside these ranges and needn't reach their ends.
All inputs are finite; a program needn't handle non-finite values.
Results may differ from the reference program's by a relative error of at most 0.006.
Values may be sent and summed in bfloat16 or wider, within the bound.
No kernel may reach another device: no remote copies, remote signals or barrier semaphores. Data moves between devices by JAX's collectives and lax.ppermute only.
A program may use at most 64 MiB of HBM per device.

```python
import math
import jax
import jax.numpy as jnp
from jax import lax

D = 2048
H = 16
HS = 128
COLS = 1024
ROWS = 32
TOKENS = 32768


def draw_signal(key, part):
    first_key, second_key, third_key = jax.random.split(key, 3)
    position = jnp.arange(D, dtype=jnp.float32) / (D - 1)
    feature = jnp.exp(position * math.log(3.0)) * jax.random.uniform(second_key, (D,), jnp.float32, 0.7, 1.0)
    entries = jnp.clip(jax.random.normal(first_key, (TOKENS, D), jnp.float32), -4.0, 4.0)
    row_scale = jnp.exp(jax.random.uniform(third_key, (TOKENS, 1), jnp.float32, math.log(0.3), math.log(3.0)))
    return (entries * row_scale * feature).astype(jnp.bfloat16)


def draw_qkv_weight(key, part):
    first_key = jax.random.fold_in(key, 0)
    entries = jnp.clip(jax.random.normal(first_key, (D, H, 3, HS), jnp.float32), -4.0, 4.0) / math.sqrt(D)
    return entries.reshape(D, 3 * D).astype(jnp.bfloat16)


def steps_of(key, dims, cuts, smallest, high):
    def one(axis_at, blocks):
        steps = jax.random.uniform(jax.random.fold_in(jax.random.fold_in(key, 6), axis_at), (blocks,), jnp.float32, smallest / len(cuts), high / len(cuts))
        return jnp.repeat(jnp.exp(steps), dims[axis_at] // blocks).reshape((-1,) + (1,) * (len(dims) - axis_at - 1))

    factor_of = one(*cuts[0])
    for cut in cuts[1:]:
        factor_of = factor_of * one(*cut)
    return factor_of


def centred(rng, dims, spread, most, pieces=(), held_as=jnp.bfloat16):
    result = spread * jax.random.normal(rng, dims, jnp.float32)
    if pieces:
        result = result * steps_of(rng, dims, pieces, -0.22, 0.18)
    return jnp.clip(result, -most, most).astype(held_as)


def setup_inputs(seed: int = 0) -> dict:
    seeds = jax.random.split(jax.random.key(seed), 5)
    return {
        "signal": draw_signal(jax.random.fold_in(seeds[4], 71), 0),
        "norm_gain": jnp.clip(jnp.exp(jax.random.uniform(seeds[1], (D,), jnp.float32, math.log(0.5), math.log(2.0))), 0.5, 2.0),
        "qkv_weight": draw_qkv_weight(jax.random.fold_in(seeds[4], 71), 0),
        "out_weight": centred(seeds[3], (D, D), (D // 64) ** -0.5, 1.0, ((0, 16), (1, 16))),
    }


EPSILON = 1e-05
NEGATIVE = -1e+30

def reference(signal, norm_gain, qkv_weight, out_weight):
    widened = signal.astype(jnp.float32)
    average = lax.optimization_barrier(jnp.mean(widened, axis=1, keepdims=True))
    variance = lax.optimization_barrier(jnp.mean((widened - average) ** 2, axis=1, keepdims=True))
    normed = ((widened - average) * lax.rsqrt(variance + EPSILON) * norm_gain).astype(jnp.bfloat16)
    qkv = jnp.dot(normed, qkv_weight, preferred_element_type=jnp.float32).astype(jnp.bfloat16)
    qkv = qkv.reshape(ROWS, COLS, H, 3, HS)
    factor = 1.0 / math.sqrt(HS)

    def row_softmax(row_block):
        queries = row_block[:, :, 0].astype(jnp.float32)
        key_part = row_block[:, :, 1].astype(jnp.float32)
        values = row_block[:, :, 2].astype(jnp.float32)
        scores = jnp.einsum('chd,ehd->hce', queries, key_part) * factor
        causal = jnp.arange(COLS)[:, None] >= jnp.arange(COLS)[None, :]
        scores = jnp.where(causal, scores, NEGATIVE)
        maxima = lax.optimization_barrier(jnp.max(scores, axis=-1))
        weights = jnp.where(causal, jnp.exp(scores - maxima[..., None]), 0.0)
        totals = lax.optimization_barrier(jnp.sum(weights, axis=-1))
        rounded = lax.optimization_barrier(weights.astype(jnp.bfloat16)).astype(jnp.float32)
        summed = jnp.einsum('hce,ehd->chd', rounded, values)
        return (summed, maxima.T, totals.T)
    row_acc, row_max, row_total = lax.map(row_softmax, qkv)
    queries = qkv[:, :, :, 0].astype(jnp.float32)
    key_part = qkv[:, :, :, 1].astype(jnp.float32)
    values = qkv[:, :, :, 2].astype(jnp.float32)
    scores = jnp.einsum('rchd,schd->chrs', queries, key_part) * factor
    earlier = jnp.arange(ROWS)[:, None] > jnp.arange(ROWS)[None, :]
    scores = jnp.where(earlier, scores, NEGATIVE)
    maxima = lax.optimization_barrier(jnp.max(scores, axis=-1))
    weights = jnp.where(earlier, jnp.exp(scores - maxima[..., None]), 0.0)
    totals = lax.optimization_barrier(jnp.sum(weights, axis=-1))
    rounded = lax.optimization_barrier(weights.astype(jnp.bfloat16)).astype(jnp.float32)
    col_acc = jnp.einsum('chrs,schd->rchd', rounded, values)
    col_max = jnp.transpose(maxima, (2, 0, 1))
    col_total = jnp.transpose(totals, (2, 0, 1))
    highest = jnp.maximum(row_max, col_max)
    row_factor = jnp.exp(row_max - highest)
    col_factor = jnp.exp(col_max - highest)
    denominator = row_factor * row_total + col_factor * col_total
    merged = (row_factor[..., None] * row_acc + col_factor[..., None] * col_acc) / denominator[..., None]
    attended = merged.astype(jnp.bfloat16).reshape(ROWS * COLS, H * HS)
    branch = jnp.dot(attended, out_weight, preferred_element_type=jnp.float32)
    return (widened + branch).astype(jnp.bfloat16)
```

```python
import functools
import math

import jax
import jax.numpy as jnp
from jax import lax
from jax.experimental import pallas as pl
from jax.experimental.pallas import tpu as pltpu
from jax.sharding import PartitionSpec as P

HS = 128
COLS = 1024
EPSILON = 1e-05
NEGATIVE = -1e30
LOG2E = math.log2(math.e)
SCALE2 = LOG2E / math.sqrt(HS)

BF16 = jnp.bfloat16
F32 = jnp.float32


def _col(z, y, c):
    return (z % 2) * 8 + (y % 4) * 2 + c


def _over_col(x, to):
    pairs = [(_col(z, y, c), to(z, y, c)) for z in range(2) for y in range(4) for c in range(2)]
    return lax.ppermute(x, "col", pairs)


def _over_row(x, to):
    pairs = [(z * 4 + h, to(z, h)) for z in range(4) for h in range(4)]
    return lax.ppermute(x, "row", pairs)


def y_up(x):
    return _over_col(x, lambda z, y, c: _col(z, y + 1, c))


def y_down(x):
    return _over_col(x, lambda z, y, c: _col(z, y + 3, c))


def z_swap(x):
    return _over_col(x, lambda z, y, c: _col(z + 1, y, c))


def core_swap(x):
    return _over_col(x, lambda z, y, c: _col(z, y, 1 - c))


def zh_shift(x, d):
    return _over_row(x, lambda z, h: ((z + d) % 4) * 4 + h)


def x_shift(x, d):
    return _over_row(x, lambda z, h: z * 4 + (h + d) % 4)


def gather_chips(x):
    n = x.shape[0] // 2
    a = y_up(x)
    b = y_down(x)
    p = z_swap(x)
    f_top = y_up(a[:n])
    f_low = y_down(b[n:])
    pa = y_up(p)
    pb = y_down(p)
    g_top = z_swap(f_top)
    g_low = z_swap(f_low)
    return (x, a, b, p, pa, pb, f_top, f_low, g_top, g_low)


WHOLE = ((0, 0), (0, 3), (0, 1), (1, 0), (1, 3), (1, 1))
HALVED = ((0, 2), (1, 2))


def gather_weights(w):
    z = jnp.stack([w] + [zh_shift(w, d) for d in (1, 2, 3)])
    n = w.shape[0] // 2
    a = x_shift(z, 1)
    b = x_shift(z, 3)
    f_top = x_shift(a[:, :n], 1)
    f_low = x_shift(b[:, n:], 3)
    pieces = (z, a, b, f_top, f_low)
    swapped = [core_swap(t) for t in pieces]

    def stacked(t):
        return jnp.stack([t[0], t[1], jnp.concatenate([t[3], t[4]], axis=1), t[2]])

    return stacked(pieces), stacked(swapped)


def _weight(ref, block, place, columns):
    z, x = place[2], place[3]
    dz = lax.rem(z + 4 - block // 4, 4)
    dx = lax.rem(x + 4 - lax.rem(block, 4), 4)
    return ref[dx, dz, :, columns]


def _pieces(refs, place, tile, start, rows):
    zl, y = place[0], place[1]
    out = []
    for ref, (dz, dy) in zip(refs[:6], WHOLE):
        j = lax.rem(zl + dz, 2) * 4 + lax.rem(y + dy, 4)
        out.append((ref[pl.ds(start, rows), :], j))
    half = refs[6].shape[0]
    for n, (dz, dy) in enumerate(HALVED):
        j = lax.rem(zl + dz, 2) * 4 + lax.rem(y + dy, 4)
        ref = refs[6 + 2 * n] if tile * rows < half else refs[7 + 2 * n]
        out.append((ref[pl.ds(start % half, rows), :], j))
    return out


def _qkv_kernel(place, gain_ref, *refs):
    pieces, (own_w, other_w, own_ref, other_ref) = refs[:10], refs[10:]
    rows = 256
    width = own_ref.shape[1]
    for tile in range(own_ref.shape[0] // rows):
        got = _pieces(pieces, place, tile, tile * rows, rows)
        total = sum(jnp.sum(v.astype(F32), axis=1, keepdims=True) for v, _ in got)
        mean = total * (1.0 / 2048)
        square = sum(jnp.sum((v.astype(F32) - mean) ** 2, axis=1, keepdims=True) for v, _ in got)
        rstd = lax.rsqrt(square * (1.0 / 2048) + EPSILON)
        own = jnp.zeros((rows, width), F32)
        other = jnp.zeros((rows, width), F32)
        for v, j in got:
            gain = gain_ref[pl.ds(j, 1), :]
            normed = ((v.astype(F32) - mean) * rstd * gain).astype(BF16)
            for h in range(2):
                part = normed[:, h * 128 : (h + 1) * 128]
                block = 2 * j + h
                other += jnp.dot(
                    part, _weight(other_w, block, place, pl.ds(0, width)), preferred_element_type=F32
                )
                own += jnp.dot(
                    part, _weight(own_w, block, place, pl.ds(0, width)), preferred_element_type=F32
                )
        own_ref[pl.ds(tile * rows, rows), :] = own.astype(BF16)
        other_ref[pl.ds(tile * rows, rows), :] = other.astype(BF16)


def _out_kernel(place, x_ref, *refs):
    pieces, (own_w, other_w, own_ref, other_ref) = refs[:10], refs[10:]
    rows = 256
    core = place[4]
    for tile in range(own_ref.shape[0] // rows):
        got = _pieces(pieces, place, tile, tile * rows, rows)
        own = jnp.zeros((rows, HS), F32)
        other = jnp.zeros((rows, HS), F32)
        for v, j in got:
            for h in range(2):
                part = v[:, h * 128 : (h + 1) * 128]
                block = 2 * j + h
                other += jnp.dot(
                    part, _weight(other_w, block, place, pl.ds(384, HS)), preferred_element_type=F32
                )
                own += jnp.dot(
                    part, _weight(own_w, block, place, pl.ds(384, HS)), preferred_element_type=F32
                )
        left = x_ref[pl.ds(tile * rows, rows), pl.ds(0, HS)].astype(F32)
        right = x_ref[pl.ds(tile * rows, rows), pl.ds(HS, HS)].astype(F32)
        first = core == 0
        own_ref[pl.ds(tile * rows, rows), :] = (jnp.where(first, left, right) + own).astype(BF16)
        other_ref[pl.ds(tile * rows, rows), :] = (jnp.where(first, right, left) + other).astype(BF16)


def _row_kernel(a_ref, b_ref, out_ref, lse_ref):
    rows = 256
    diagonal = lax.broadcasted_iota(jnp.int32, (rows, rows), 0) >= lax.broadcasted_iota(
        jnp.int32, (rows, rows), 1
    )
    for n, ref in enumerate((a_ref, b_ref)):
        for tile in range(COLS // rows):
            lo, hi = tile * rows, (tile + 1) * rows
            q = ref[lo:hi, 0:HS]
            nt = (((1,), (1,)), ((), ()))
            last = lax.dot_general(q, ref[lo:hi, HS : 2 * HS], nt, preferred_element_type=F32)
            last = jnp.where(diagonal, last, NEGATIVE)
            top = jnp.max(last, axis=1, keepdims=True)
            if tile:
                before = lax.dot_general(q, ref[0:lo, HS : 2 * HS], nt, preferred_element_type=F32)
                top = jnp.maximum(top, jnp.max(before, axis=1, keepdims=True))
            w = jnp.exp2((last - top) * SCALE2)
            total = jnp.sum(w, axis=1, keepdims=True)
            acc = jnp.dot(w.astype(BF16), ref[lo:hi, 2 * HS :], preferred_element_type=F32)
            if tile:
                w = jnp.exp2((before - top) * SCALE2)
                total += jnp.sum(w, axis=1, keepdims=True)
                acc += jnp.dot(w.astype(BF16), ref[0:lo, 2 * HS :], preferred_element_type=F32)
            out_ref[n, lo:hi, :] = acc / total
            lse_ref[n, lo:hi, :] = top * SCALE2 + jnp.log2(total)


def _column_kernel(place, z_ref, out_ref):
    core = place[4]
    g_cols = 16
    n = 16 * g_cols
    t = 2 * n

    def facts(dim, shape):
        i = lax.broadcasted_iota(jnp.int32, shape, dim)
        second = i // n
        source = lax.rem(i, n) // g_cols
        column = lax.rem(i, g_cols)
        parity = jnp.where(second == 1, 1 - core, core)
        return second, source, column, 2 * source + parity

    _, _, qc, qr = facts(0, (t, t))
    _, _, kc, kr = facts(1, (t, t))
    valid = (qc == kc) & (qr > kr)
    second, _, column, row = facts(0, (t, 1))
    lane = lax.broadcasted_iota(jnp.int32, (t, 128), 1)
    home = column + second * 64
    dest = lax.broadcasted_iota(jnp.int32, (256, t), 0)
    _, source, _, _ = facts(1, (256, t))
    picks = [(dest == source * 16 + m).astype(F32).astype(BF16) for m in range(3)]
    stats = jnp.zeros((256, 128), F32)
    for g in range(64 // g_cols):
        one = z_ref[:, g * g_cols : (g + 1) * g_cols, :].reshape(n, 3 * HS)
        two = z_ref[:, 64 + g * g_cols : 64 + (g + 1) * g_cols, :].reshape(n, 3 * HS)
        both = jnp.concatenate([one, two], axis=0)
        s = lax.dot_general(
            both[:, 0:HS], both[:, HS : 2 * HS], (((1,), (1,)), ((), ())), preferred_element_type=F32
        )
        s = jnp.where(valid, s, NEGATIVE)
        top = jnp.max(s, axis=1, keepdims=True)
        w = jnp.where(valid, jnp.exp2((s - top) * SCALE2), 0.0)
        total = jnp.sum(w, axis=1, keepdims=True)
        acc = jnp.dot(w.astype(BF16), both[:, 2 * HS :], preferred_element_type=F32)
        some = row > 0
        safe = jnp.where(some, total, 1.0)
        o = (acc / safe).astype(BF16)
        lse = jnp.where(some, top * SCALE2 + jnp.log2(safe), NEGATIVE)
        out_ref[:, g * g_cols : (g + 1) * g_cols, :] = o[:n].reshape(16, g_cols, HS)
        out_ref[:, 64 + g * g_cols : 64 + (g + 1) * g_cols, :] = o[n:].reshape(16, g_cols, HS)
        here = lane == home + g * g_cols
        rest = lse
        for pick in picks:
            part = rest.astype(BF16).astype(F32)
            rest = rest - part
            spread = jnp.where(here, part, 0.0).astype(BF16)
            stats += jnp.dot(pick, spread, preferred_element_type=F32)
    out_ref[:, 128:144, :] = stats.astype(BF16).reshape(16, 16, 128)


def _merge_kernel(row_ref, lse_ref, col_ref, own_ref, other_ref):
    eye = (
        lax.broadcasted_iota(jnp.int32, (128, 128), 0) == lax.broadcasted_iota(jnp.int32, (128, 128), 1)
    )
    eye = eye.astype(F32).astype(BF16)
    for src in range(16):
        parts = lax.dot_general(
            eye, col_ref[src, 128:144, :], (((1,), (1,)), ((), ())), preferred_element_type=F32
        )
        col_lse = parts[:, 0:1] + parts[:, 1:2] + parts[:, 2:3]
        for n, ref in enumerate((own_ref, other_ref)):
            at = src * 64
            cl = col_lse[n * 64 : (n + 1) * 64]
            rl = lse_ref[n, at : at + 64, :]
            top = jnp.maximum(cl, rl)
            rf = jnp.exp2(rl - top)
            cf = jnp.exp2(cl - top)
            o = rf * row_ref[n, at : at + 64, :] + cf * col_ref[src, n * 64 : (n + 1) * 64, :].astype(F32)
            ref[at : at + 64, :] = (o / (rf + cf)).astype(BF16)


def _call(kernel, name, out, *args, scalars=0):
    vmem = pl.BlockSpec(memory_space=pltpu.VMEM)
    smem = pl.BlockSpec(memory_space=pltpu.SMEM)
    return pl.pallas_call(
        kernel,
        name=name,
        out_shape=out,
        in_specs=[smem] * scalars + [vmem] * (len(args) - scalars),
        out_specs=jax.tree.map(lambda _: vmem, out),
    )(*args)


def per_device(signal, norm_gain, qkv_weight, out_weight):
    shape = jax.ShapeDtypeStruct
    r = lax.axis_index("row")
    c = lax.axis_index("col")
    core = c % 2
    place = jnp.stack([c // 8, (c // 2) % 4, r // 4, r % 4, core]).astype(jnp.int32)

    mine = lax.dynamic_slice_in_dim(signal, core * COLS, COLS, 0)
    theirs = core_swap(lax.dynamic_slice_in_dim(signal, (1 - core) * COLS, COLS, 0))
    first = core == 0

    def side_by_side(own, other):
        return jnp.where(
            first, jnp.concatenate([own, other], axis=1), jnp.concatenate([other, own], axis=1)
        )

    x = side_by_side(mine, theirs)
    pieces = gather_chips(x)
    own_w, other_w = gather_weights(jnp.concatenate([qkv_weight, out_weight], axis=1))

    half = shape((COLS, 3 * HS), BF16)
    qkv_a, qkv_other = _call(
        _qkv_kernel,
        "qkv",
        (half, half),
        place,
        norm_gain.reshape(8, 256),
        *pieces,
        own_w,
        other_w,
        scalars=1,
    )
    qkv_b = core_swap(qkv_other)
    by_column = jnp.concatenate([qkv_a.reshape(16, 64, 3 * HS), qkv_b.reshape(16, 64, 3 * HS)], axis=1)
    by_column = lax.all_to_all(by_column, "row", split_axis=0, concat_axis=0, tiled=True)
    row_out, row_lse = _call(
        _row_kernel, "row_attention", (shape((2, COLS, HS), F32), shape((2, COLS, 1), F32)), qkv_a, qkv_b
    )
    col_out = _call(_column_kernel, "column_attention", shape((16, 144, HS), BF16), place, by_column, scalars=1)
    col_out = lax.all_to_all(col_out, "row", split_axis=0, concat_axis=0, tiled=True)
    one = shape((COLS, HS), BF16)
    att_own, att_other = _call(_merge_kernel, "merge", (one, one), row_out, row_lse, col_out)
    att = side_by_side(att_own, core_swap(att_other))
    out_own, out_other = _call(
        _out_kernel, "out", (one, one), place, x, *gather_chips(att), own_w, other_w, scalars=1
    )
    back = core_swap(out_other)
    return jnp.where(
        first, jnp.concatenate([out_own, back], axis=0), jnp.concatenate([back, out_own], axis=0)
    )


def solution(mesh):
    return jax.shard_map(
        per_device,
        mesh=mesh,
        in_specs=(P("row", "col"), P(), P("row", "col"), P("row", "col")),
        out_specs=P("row", "col"),
        check_vma=False,
    )
```

```python
import math

import jax
import jax.numpy as jnp
from jax import lax
from jax.experimental import pallas as pl
from jax.experimental.pallas import tpu as pltpu
from jax.sharding import PartitionSpec as P


HS = 128
COLS = 1024
EPSILON = 1e-05
NEGATIVE = -1e30
SCALE2 = math.log2(math.e) / math.sqrt(HS)
TILE = 256
G_COLS = 16
STAT_ROWS = 8

BF16 = jnp.bfloat16
F32 = jnp.float32
NT = (((1,), (1,)), ((), ()))


def _col(z, y, c):
    return (z % 2) * 8 + (y % 4) * 2 + c


def _over_col(x, to):
    pairs = [(_col(z, y, c), to(z, y, c)) for z in range(2) for y in range(4) for c in range(2)]
    return lax.ppermute(x, "col", pairs)


def _over_row(x, to):
    pairs = [(z * 4 + h, to(z, h)) for z in range(4) for h in range(4)]
    return lax.ppermute(x, "row", pairs)


def y_up(x):
    return _over_col(x, lambda z, y, c: _col(z, y + 1, c))


def y_down(x):
    return _over_col(x, lambda z, y, c: _col(z, y + 3, c))


def z_swap(x):
    return _over_col(x, lambda z, y, c: _col(z + 1, y, c))


def core_swap(x):
    return _over_col(x, lambda z, y, c: _col(z, y, 1 - c))


def zh_shift(x, d):
    return _over_row(x, lambda z, h: ((z + d) % 4) * 4 + h)


def x_shift(x, d):
    return _over_row(x, lambda z, h: z * 4 + (h + d) % 4)


def gather_chips(x):
    a = y_up(x)
    b = y_down(x)
    p = z_swap(x)
    left = a[:, :HS]
    fl = y_up(left)
    fr = y_down(b[:, HS:])
    pa = y_up(p)
    pb = y_down(p)
    gl = z_swap(fl)
    gr = z_swap(fr)
    return (x, b, fl, fr, a, p, pb, gl, gr, pa)


def over_z_hi(w):
    return jnp.stack([w] + [zh_shift(w, d) for d in (1, 2, 3)])


def over_x(z):
    return (z, *(x_shift(z, d) for d in (1, 2, 3)))


def _weights_kernel(place, *refs):
    out = refs[-1]
    sides = len(refs) // 4
    width = out.shape[1] // sides
    zl, y, zh, x = place[0], place[1], place[2], place[3]
    for dx in range(4):
        for dz in range(4):
            block = lax.rem(zh + 4 - dz, 4) * 4 + lax.rem(x + 4 - dx, 4)
            chip, half = block // 2, lax.rem(block, 2)
            piece = lax.rem(chip // 4 + zl, 2) * 4 + lax.rem(lax.rem(chip, 4) + 4 - y, 4)
            at = pl.multiple_of(piece * 256 + half * 128, 128)
            for side in range(sides):
                out[pl.ds(at, 128), side * width : (side + 1) * width] = refs[4 * side + dx][dz]


def _qkv_kernel(place, gain_ref, *refs):
    pieces, (w_ref, out_ref, even_ref, odd_ref) = refs[:10], refs[10:]
    zl, y, core = place[0], place[1], place[4]
    gains = []
    for i in range(8):
        j = lax.rem(zl + i // 4, 2) * 4 + lax.rem(y + i, 4)
        gains.append(gain_ref[pl.ds(j, 1), :])
    gain = jnp.concatenate(gains, axis=1)
    wide = 2048
    chunks = []
    lane = 0
    for ref in pieces:
        for k in range(ref.shape[1] // HS):
            chunks.append((ref, k * HS, lane))
            lane += HS

    def rows_of(tile):
        return pl.ds(pl.multiple_of(tile * TILE, TILE), TILE)

    def mean_of(tile):
        total = jnp.zeros((TILE, HS), F32)
        for ref, k, _ in chunks:
            total += ref[rows_of(tile), pl.ds(k, HS)].astype(F32)
        return jnp.sum(total, axis=1, keepdims=True) * (1.0 / wide)

    def rstd_of(tile, mean):
        square = jnp.zeros((TILE, HS), F32)
        for ref, k, _ in chunks:
            v = ref[rows_of(tile), pl.ds(k, HS)].astype(F32) - mean
            square += v * v
        return lax.rsqrt(jnp.sum(square, axis=1, keepdims=True) * (1.0 / wide) + EPSILON)

    def norm(tile, mean, rstd, to_ref):
        for ref, k, at in chunks:
            v = ref[rows_of(tile), pl.ds(k, HS)].astype(F32) - mean
            to_ref[:, pl.ds(at, HS)] = (v * rstd * gain[:, at : at + HS]).astype(BF16)

    def project(tile, from_ref, part):
        lanes = pl.ds(part * HS * 2, HS * 2)
        qkv = jnp.dot(from_ref[...], w_ref[:, lanes], preferred_element_type=F32).astype(BF16)
        blocks = pl.ds(tile * (TILE // 64), TILE // 64)
        for k in range(2):
            n = 2 * part + k
            slot = core if n < 3 else 1 - core
            v = qkv[:, k * HS : (k + 1) * HS].reshape(TILE // 64, 64, HS)
            out_ref[blocks, slot, :, (n % 3) * HS : (n % 3 + 1) * HS] = v

    def both(tile, from_ref, later, to_ref):
        mean = mean_of(later)
        project(tile, from_ref, 0)
        rstd = rstd_of(later, mean)
        project(tile, from_ref, 1)
        norm(later, mean, rstd, to_ref)
        project(tile, from_ref, 2)

    count = COLS // TILE
    mean = mean_of(0)
    norm(0, mean, rstd_of(0, mean), even_ref)

    def step(i, carry):
        both(2 * i, even_ref, 2 * i + 1, odd_ref)
        both(2 * i + 1, odd_ref, jnp.minimum(2 * i + 2, count - 1), even_ref)
        return carry

    lax.fori_loop(0, count // 2, step, 0)


def _out_kernel(place, x_ref, *refs):
    pieces, (w_ref, own_ref, other_ref) = refs[:10], refs[10:]
    core = place[4]

    for tile in range(COLS // TILE):
        at = tile * TILE
        v = jnp.concatenate([ref[pl.ds(at, TILE), :] for ref in pieces], axis=1)
        branch = jnp.dot(v, w_ref[...], preferred_element_type=F32)
        left = x_ref[pl.ds(at, TILE), pl.ds(0, HS)].astype(F32)
        right = x_ref[pl.ds(at, TILE), pl.ds(HS, HS)].astype(F32)
        own = jnp.where(core == 0, left, right) + branch[:, :HS]
        other = jnp.where(core == 0, right, left) + branch[:, HS:]
        own_ref[pl.ds(pl.multiple_of(core * COLS + at, TILE), TILE), :] = own.astype(BF16)
        other_ref[pl.ds(at, TILE), :] = other.astype(BF16)


def _row_kernel(head, qkv_ref, out_ref, lse_ref):
    diagonal = lax.broadcasted_iota(jnp.int32, (TILE, TILE), 0) >= lax.broadcasted_iota(
        jnp.int32, (TILE, TILE), 1
    )
    n = TILE // 64
    lane = lax.broadcasted_iota(jnp.int32, (64, HS), 1)
    packed = jnp.zeros((64, HS), F32)

    def part(lo, hi, k):
        v = qkv_ref[lo * n : hi * n, head, :, k * HS : (k + 1) * HS]
        return v.reshape((hi - lo) * TILE, HS)

    for tile in range(COLS // TILE):
        q = part(tile, tile + 1, 0)
        last = lax.dot_general(q, part(tile, tile + 1, 1), NT, preferred_element_type=F32)
        last = jnp.where(diagonal, last, NEGATIVE)
        top = jnp.max(last, axis=1, keepdims=True)
        if tile:
            before = lax.dot_general(q, part(0, tile, 1), NT, preferred_element_type=F32)
            top = jnp.maximum(top, jnp.max(before, axis=1, keepdims=True))
        w = jnp.exp2((last - top) * SCALE2)
        total = jnp.sum(w, axis=1, keepdims=True)
        acc = jnp.dot(w.astype(BF16), part(tile, tile + 1, 2), preferred_element_type=F32)
        if tile:
            w = jnp.exp2((before - top) * SCALE2)
            total += jnp.sum(w, axis=1, keepdims=True)
            acc += jnp.dot(w.astype(BF16), part(0, tile, 2), preferred_element_type=F32)
        out_ref[tile * TILE : (tile + 1) * TILE, :] = acc / total
        lse = top * SCALE2 + jnp.log2(total)
        for k in range(n):
            here = lane == 2 * (tile * n + k) + head
            packed = jnp.where(here, lse[k * 64 : (k + 1) * 64], packed)
    lse_ref[...] = packed


def _column_kernel(z_ref, out_ref):
    t = 32 * G_COLS
    i = lax.broadcasted_iota(jnp.int32, (t, t), 0)
    j = lax.broadcasted_iota(jnp.int32, (t, t), 1)
    valid = (lax.rem(i, G_COLS) == lax.rem(j, G_COLS)) & (i > j)
    bias = jnp.where(valid, 0.0, NEGATIVE)
    token = lax.broadcasted_iota(jnp.int32, (t, 1), 0)
    lane = lax.broadcasted_iota(jnp.int32, (t, HS), 1) - lax.rem(token, G_COLS)
    dest = lax.broadcasted_iota(jnp.int32, (32 * STAT_ROWS, t), 0)
    source = lax.broadcasted_iota(jnp.int32, (32 * STAT_ROWS, t), 1) // G_COLS
    picks = [(dest == source * STAT_ROWS + m).astype(F32).astype(BF16) for m in range(3)]

    spread = jnp.zeros((t, HS), F32)
    for g in range(64 // G_COLS):
        at = g * G_COLS
        z = z_ref[:, at : at + G_COLS, :].reshape(t, 3 * HS)
        s = lax.dot_general(z[:, :HS], z[:, HS : 2 * HS], NT, preferred_element_type=F32) + bias
        top = jnp.max(s, axis=1, keepdims=True)
        w = jnp.exp2((s - top) * SCALE2)
        total = jnp.sum(w, axis=1, keepdims=True)
        acc = jnp.dot(w.astype(BF16), z[:, 2 * HS :], preferred_element_type=F32)
        out_ref[:, at : at + G_COLS, :] = (acc / total).astype(BF16).reshape(32, G_COLS, HS)
        lse = jnp.where(token >= G_COLS, top * SCALE2 + jnp.log2(total), NEGATIVE)
        spread = jnp.where(lane == at, lse, spread)
    stats = jnp.zeros((32 * STAT_ROWS, HS), F32)
    for pick in picks:
        part = spread.astype(BF16)
        spread = spread - part.astype(F32)
        stats += jnp.dot(pick, part, preferred_element_type=F32)
    out_ref[:, 64 : 64 + STAT_ROWS, :] = stats.astype(BF16).reshape(32, STAT_ROWS, HS)


def _merge_kernel(row0_ref, lse0_ref, row1_ref, lse1_ref, col_ref, out_ref):
    stats = col_ref[:, :, 64:, :].reshape(32 * STAT_ROWS, HS)
    source = lax.broadcasted_iota(jnp.int32, (HS, 32 * STAT_ROWS), 1)
    entry = lax.broadcasted_iota(jnp.int32, (HS, 32 * STAT_ROWS), 0)
    picks = [(source == entry * STAT_ROWS + m).astype(F32).astype(BF16) for m in range(3)]
    parts = [jnp.dot(pick, stats, preferred_element_type=F32) for pick in picks]
    cl = (parts[0] + parts[1] + parts[2]).T[:64]
    rl = lse0_ref[...] + lse1_ref[...]
    top = jnp.maximum(cl, rl)
    rf = jnp.exp2(rl - top)
    cf = jnp.exp2(cl - top)
    share = 1.0 / (rf + cf)
    rf = rf * share
    cf = cf * share
    for block in range(16):
        rows = slice(block * 64, (block + 1) * 64)
        for head, row_ref in enumerate((row0_ref, row1_ref)):
            n = 2 * block + head
            o = rf[:, n : n + 1] * row_ref[rows, :] + cf[:, n : n + 1] * col_ref[block, head, :64, :].astype(F32)
            out_ref[rows, head * HS : (head + 1) * HS] = o.astype(BF16)


def _call(kernel, out, *args, scalars=0, flops=0, scratch=(), mib=24):
    vmem = pl.BlockSpec(memory_space=pltpu.VMEM)
    smem = pl.BlockSpec(memory_space=pltpu.SMEM)
    cost = pl.CostEstimate(flops=flops, transcendentals=0, bytes_accessed=1 << 20) if flops else None
    return pl.pallas_call(
        kernel,
        out_shape=out,
        in_specs=[smem] * scalars + [vmem] * (len(args) - scalars),
        out_specs=jax.tree.map(lambda _: vmem, out),
        cost_estimate=cost,
        scratch_shapes=scratch,
        compiler_params=pltpu.CompilerParams(vmem_limit_bytes=mib << 20),
    )(*args)


CHIP_GROUPS = [[r * 16 + 2 * j + k for r in range(16) for k in range(2)] for j in range(8)]


def exchange_columns(x):
    return lax.all_to_all(
        x, ("row", "col"), split_axis=0, concat_axis=0, axis_index_groups=CHIP_GROUPS, tiled=True
    )


def per_device(signal, norm_gain, qkv_weight, out_weight):
    shape = jax.ShapeDtypeStruct
    r = lax.axis_index("row")
    c = lax.axis_index("col")
    core = lax.rem(c, 2)
    place = jnp.stack([lax.div(c, 8), lax.rem(lax.div(c, 2), 4), lax.div(r, 4), lax.rem(r, 4), core])

    mine = lax.dynamic_slice_in_dim(signal, core * COLS, COLS, 0)
    theirs = core_swap(lax.dynamic_slice_in_dim(signal, (1 - core) * COLS, COLS, 0))
    x = jnp.where(
        core == 0, jnp.concatenate([mine, theirs], axis=1), jnp.concatenate([theirs, mine], axis=1)
    )
    weights = jnp.concatenate([qkv_weight, out_weight], axis=1)
    pieces = gather_chips(x)
    weights = over_z_hi(weights)
    own = over_x(weights[..., : 3 * HS])
    other = (core_swap(t) for t in own)
    w = _call(_weights_kernel, shape((2048, 6 * HS), BF16), place, *own, *other, scalars=1)
    qkv = _call(
        _qkv_kernel,
        shape((16, 2, 64, 3 * HS), BF16),
        place,
        norm_gain.reshape(8, 256),
        *pieces,
        w,
        scalars=1,
        scratch=[pltpu.VMEM((TILE, 2048), BF16)] * 2,
    )
    by_column = exchange_columns(qkv.reshape(32, 64, 3 * HS))
    weights, qkv = lax.optimization_barrier((weights[..., 3 * HS :], qkv))
    w = _call(_weights_kernel, shape((2048, HS), BF16), place, *over_x(weights), scalars=1)
    w = jnp.concatenate([w, core_swap(w)], axis=1)
    row = []
    for head in range(2):
        row += _call(
            lambda *refs, head=head: _row_kernel(head, *refs),
            (shape((COLS, HS), F32), shape((64, HS), F32)),
            qkv,
            flops=1 << 33,
        )
    by_column, w, first = lax.optimization_barrier((by_column, w, tuple(row[:2])))
    col_out = _call(_column_kernel, shape((32, 64 + STAT_ROWS, HS), BF16), by_column)
    col_out = exchange_columns(col_out).reshape(16, 2, 64 + STAT_ROWS, HS)
    att = _call(_merge_kernel, shape((COLS, 2 * HS), BF16), *first, *row[2:], col_out)
    out_own, out_other = _call(
        _out_kernel, (shape((2 * COLS, HS), BF16), shape((COLS, HS), BF16)), place, x, *gather_chips(att), w, scalars=1
    )
    return lax.dynamic_update_slice_in_dim(out_own, core_swap(out_other), (1 - core) * COLS, 0)


def solution(mesh):
    return jax.shard_map(
        per_device,
        mesh=mesh,
        in_specs=(P("row", "col"), P(), P("row", "col"), P("row", "col")),
        out_specs=P("row", "col"),
        check_vma=False,
    )
```

```python
import math

import jax
import jax.numpy as jnp
from jax import lax
from jax.experimental import pallas as pl
from jax.experimental.pallas import tpu as pltpu
from jax.sharding import PartitionSpec as P


HS = 128
COLS = 1024
EPSILON = 1e-05
NEGATIVE = -1e30
SCALE2 = math.log2(math.e) / math.sqrt(HS)
TILE = 256
G_COLS = 16
STAT_ROWS = 8

BF16 = jnp.bfloat16
F32 = jnp.float32
NT = (((1,), (1,)), ((), ()))


def _col(z, y, c):
    return (z % 2) * 8 + (y % 4) * 2 + c


def _over_col(x, to):
    pairs = [(_col(z, y, c), to(z, y, c)) for z in range(2) for y in range(4) for c in range(2)]
    return lax.ppermute(x, "col", pairs)


def _over_row(x, to):
    pairs = [(z * 4 + h, to(z, h)) for z in range(4) for h in range(4)]
    return lax.ppermute(x, "row", pairs)


def y_up(x):
    return _over_col(x, lambda z, y, c: _col(z, y + 1, c))


def y_down(x):
    return _over_col(x, lambda z, y, c: _col(z, y + 3, c))


def z_swap(x):
    return _over_col(x, lambda z, y, c: _col(z + 1, y, c))


def core_swap(x):
    return _over_col(x, lambda z, y, c: _col(z, y, 1 - c))


def zh_shift(x, d):
    return _over_row(x, lambda z, h: ((z + d) % 4) * 4 + h)


def x_shift(x, d):
    return _over_row(x, lambda z, h: z * 4 + (h + d) % 4)


def gather_chips(x):
    a = y_up(x)
    b = y_down(x)
    p = z_swap(x)
    left = a[:, :HS]
    fl = y_up(left)
    fr = y_down(b[:, HS:])
    pa = y_up(p)
    pb = y_down(p)
    gl = z_swap(fl)
    gr = z_swap(fr)
    return (x, b, fl, fr, a, p, pb, gl, gr, pa)


def over_z_hi(w):
    return jnp.stack([w] + [zh_shift(w, d) for d in (1, 2, 3)])


def over_x(z):
    return (z, *(x_shift(z, d) for d in (1, 2, 3)))


def _weights_kernel(place, *refs):
    out = refs[-1]
    sides = len(refs) // 4
    width = out.shape[1] // sides
    zl, y, zh, x = place[0], place[1], place[2], place[3]
    for dx in range(4):
        for dz in range(4):
            block = lax.rem(zh + 4 - dz, 4) * 4 + lax.rem(x + 4 - dx, 4)
            chip, half = block // 2, lax.rem(block, 2)
            piece = lax.rem(chip // 4 + zl, 2) * 4 + lax.rem(lax.rem(chip, 4) + 4 - y, 4)
            at = pl.multiple_of(piece * 256 + half * 128, 128)
            for side in range(sides):
                out[pl.ds(at, 128), side * width : (side + 1) * width] = refs[4 * side + dx][dz]


def _chunks(refs):
    return [(ref, k * HS) for ref in refs for k in range(ref.shape[1] // HS)]


def _moments(chunks, rows):
    n = TILE
    total = jnp.zeros((n, HS), F32)
    for ref, k in chunks:
        total += ref[rows, pl.ds(k, HS)].astype(F32)
    mean = jnp.sum(total, axis=1, keepdims=True) * (1.0 / (len(chunks) * HS))
    square = jnp.zeros((n, HS), F32)
    for ref, k in chunks:
        v = ref[rows, pl.ds(k, HS)].astype(F32) - mean
        square += v * v
    return mean, jnp.sum(square, axis=1, keepdims=True)


EARLY = (0, 1, 2, 3, 4, 5)
LATE = (6, 7, 8, 9)
EARLY_WIDTH = 1280
LATE_WIDTH = 768


def _early_kernel(*refs):
    chunks = _chunks(refs[:-2])
    mean_ref, square_ref = refs[-2:]

    def step(tile, carry):
        rows = pl.ds(pl.multiple_of(tile * TILE, TILE), TILE)
        mean_ref[rows, :], square_ref[rows, :] = _moments(chunks, rows)
        return carry

    lax.fori_loop(0, COLS // TILE, step, 0)


def _qkv_kernel(place, gain_ref, early_mean_ref, early_square_ref, *refs):
    pieces, (w_ref, out_ref, even_ref, odd_ref) = refs[:10], refs[10:]
    zl, y, core = place[0], place[1], place[4]
    gains = []
    for i in range(8):
        j = lax.rem(zl + i // 4, 2) * 4 + lax.rem(y + i, 4)
        gains.append(gain_ref[pl.ds(j, 1), :])
    gain = jnp.concatenate(gains, axis=1)
    wide = 2048
    chunks = []
    lane = 0
    for ref in pieces:
        for k in range(ref.shape[1] // HS):
            chunks.append((ref, k * HS, lane))
            lane += HS

    def rows_of(tile):
        return pl.ds(pl.multiple_of(tile * TILE, TILE), TILE)

    late = _chunks([pieces[i] for i in LATE])

    def moments_of(tile):
        return _moments(late, rows_of(tile))

    def together(tile, late_mean, late_square):
        mean = early_mean_ref[rows_of(tile), :]
        apart = late_mean - mean
        square = early_square_ref[rows_of(tile), :] + late_square
        square += apart * apart * (EARLY_WIDTH * LATE_WIDTH / wide)
        return mean + apart * (LATE_WIDTH / wide), lax.rsqrt(square * (1.0 / wide) + EPSILON)

    def norm(tile, mean, rstd, to_ref):
        for ref, k, at in chunks:
            v = ref[rows_of(tile), pl.ds(k, HS)].astype(F32) - mean
            to_ref[:, pl.ds(at, HS)] = (v * rstd * gain[:, at : at + HS]).astype(BF16)

    def project(tile, from_ref, part):
        lanes = pl.ds(part * HS * 2, HS * 2)
        qkv = jnp.dot(from_ref[...], w_ref[:, lanes], preferred_element_type=F32).astype(BF16)
        blocks = pl.ds(tile * (TILE // 64), TILE // 64)
        for k in range(2):
            n = 2 * part + k
            slot = core if n < 3 else 1 - core
            v = qkv[:, k * HS : (k + 1) * HS].reshape(TILE // 64, 64, HS)
            out_ref[blocks, slot, :, (n % 3) * HS : (n % 3 + 1) * HS] = v

    def both(tile, from_ref, later, to_ref):
        moments = moments_of(later)
        project(tile, from_ref, 0)
        mean, rstd = together(later, *moments)
        project(tile, from_ref, 1)
        norm(later, mean, rstd, to_ref)
        project(tile, from_ref, 2)

    count = COLS // TILE
    norm(0, *together(0, *moments_of(0)), even_ref)

    def step(i, carry):
        both(2 * i, even_ref, 2 * i + 1, odd_ref)
        both(2 * i + 1, odd_ref, jnp.minimum(2 * i + 2, count - 1), even_ref)
        return carry

    lax.fori_loop(0, count // 2, step, 0)


def _out_kernel(place, x_ref, *refs):
    pieces, (w_ref, own_ref, other_ref) = refs[:10], refs[10:]
    core = place[4]

    for tile in range(COLS // TILE):
        at = tile * TILE
        v = jnp.concatenate([ref[pl.ds(at, TILE), :] for ref in pieces], axis=1)
        branch = jnp.dot(v, w_ref[...], preferred_element_type=F32)
        left = x_ref[pl.ds(at, TILE), pl.ds(0, HS)].astype(F32)
        right = x_ref[pl.ds(at, TILE), pl.ds(HS, HS)].astype(F32)
        own = jnp.where(core == 0, left, right) + branch[:, :HS]
        other = jnp.where(core == 0, right, left) + branch[:, HS:]
        own_ref[pl.ds(pl.multiple_of(core * COLS + at, TILE), TILE), :] = own.astype(BF16)
        other_ref[pl.ds(at, TILE), :] = other.astype(BF16)


def _row_kernel(head, qkv_ref, out_ref, lse_ref):
    diagonal = lax.broadcasted_iota(jnp.int32, (TILE, TILE), 0) >= lax.broadcasted_iota(
        jnp.int32, (TILE, TILE), 1
    )
    n = TILE // 64
    lane = lax.broadcasted_iota(jnp.int32, (64, HS), 1)
    packed = jnp.zeros((64, HS), F32)

    def part(lo, hi, k):
        v = qkv_ref[lo * n : hi * n, head, :, k * HS : (k + 1) * HS]
        return v.reshape((hi - lo) * TILE, HS)

    for tile in range(COLS // TILE):
        q = part(tile, tile + 1, 0)
        last = lax.dot_general(q, part(tile, tile + 1, 1), NT, preferred_element_type=F32)
        last = jnp.where(diagonal, last, NEGATIVE)
        top = jnp.max(last, axis=1, keepdims=True)
        if tile:
            before = lax.dot_general(q, part(0, tile, 1), NT, preferred_element_type=F32)
            top = jnp.maximum(top, jnp.max(before, axis=1, keepdims=True))
        w = jnp.exp2((last - top) * SCALE2)
        total = jnp.sum(w, axis=1, keepdims=True)
        acc = jnp.dot(w.astype(BF16), part(tile, tile + 1, 2), preferred_element_type=F32)
        if tile:
            w = jnp.exp2((before - top) * SCALE2)
            total += jnp.sum(w, axis=1, keepdims=True)
            acc += jnp.dot(w.astype(BF16), part(0, tile, 2), preferred_element_type=F32)
        out_ref[tile * TILE : (tile + 1) * TILE, :] = acc / total
        lse = top * SCALE2 + jnp.log2(total)
        for k in range(n):
            here = lane == 2 * (tile * n + k) + head
            packed = jnp.where(here, lse[k * 64 : (k + 1) * 64], packed)
    lse_ref[...] = packed


def _column_kernel(z_ref, out_ref):
    t = 32 * G_COLS
    i = lax.broadcasted_iota(jnp.int32, (t, t), 0)
    j = lax.broadcasted_iota(jnp.int32, (t, t), 1)
    valid = (lax.rem(i, G_COLS) == lax.rem(j, G_COLS)) & (i > j)
    bias = jnp.where(valid, 0.0, NEGATIVE)
    token = lax.broadcasted_iota(jnp.int32, (t, 1), 0)
    lane = lax.broadcasted_iota(jnp.int32, (t, HS), 1) - lax.rem(token, G_COLS)
    dest = lax.broadcasted_iota(jnp.int32, (32 * STAT_ROWS, t), 0)
    source = lax.broadcasted_iota(jnp.int32, (32 * STAT_ROWS, t), 1) // G_COLS
    picks = [(dest == source * STAT_ROWS + m).astype(F32).astype(BF16) for m in range(3)]

    spread = jnp.zeros((t, HS), F32)
    for g in range(64 // G_COLS):
        at = g * G_COLS
        z = z_ref[:, at : at + G_COLS, :].reshape(t, 3 * HS)
        s = lax.dot_general(z[:, :HS], z[:, HS : 2 * HS], NT, preferred_element_type=F32) + bias
        top = jnp.max(s, axis=1, keepdims=True)
        w = jnp.exp2((s - top) * SCALE2)
        total = jnp.sum(w, axis=1, keepdims=True)
        acc = jnp.dot(w.astype(BF16), z[:, 2 * HS :], preferred_element_type=F32)
        out_ref[:, at : at + G_COLS, :] = (acc / total).astype(BF16).reshape(32, G_COLS, HS)
        lse = jnp.where(token >= G_COLS, top * SCALE2 + jnp.log2(total), NEGATIVE)
        spread = jnp.where(lane == at, lse, spread)
    stats = jnp.zeros((32 * STAT_ROWS, HS), F32)
    for pick in picks:
        part = spread.astype(BF16)
        spread = spread - part.astype(F32)
        stats += jnp.dot(pick, part, preferred_element_type=F32)
    out_ref[:, 64 : 64 + STAT_ROWS, :] = stats.astype(BF16).reshape(32, STAT_ROWS, HS)


def _merge_kernel(row0_ref, lse0_ref, row1_ref, lse1_ref, col_ref, out_ref):
    stats = col_ref[:, :, 64:, :].reshape(32 * STAT_ROWS, HS)
    source = lax.broadcasted_iota(jnp.int32, (HS, 32 * STAT_ROWS), 1)
    entry = lax.broadcasted_iota(jnp.int32, (HS, 32 * STAT_ROWS), 0)
    picks = [(source == entry * STAT_ROWS + m).astype(F32).astype(BF16) for m in range(3)]
    parts = [jnp.dot(pick, stats, preferred_element_type=F32) for pick in picks]
    cl = (parts[0] + parts[1] + parts[2]).T[:64]
    rl = lse0_ref[...] + lse1_ref[...]
    top = jnp.maximum(cl, rl)
    rf = jnp.exp2(rl - top)
    cf = jnp.exp2(cl - top)
    share = 1.0 / (rf + cf)
    rf = rf * share
    cf = cf * share
    for block in range(16):
        rows = slice(block * 64, (block + 1) * 64)
        for head, row_ref in enumerate((row0_ref, row1_ref)):
            n = 2 * block + head
            o = rf[:, n : n + 1] * row_ref[rows, :] + cf[:, n : n + 1] * col_ref[block, head, :64, :].astype(F32)
            out_ref[rows, head * HS : (head + 1) * HS] = o.astype(BF16)


def _call(kernel, out, *args, scalars=0, flops=0, scratch=(), mib=24):
    vmem = pl.BlockSpec(memory_space=pltpu.VMEM)
    smem = pl.BlockSpec(memory_space=pltpu.SMEM)
    cost = pl.CostEstimate(flops=flops, transcendentals=0, bytes_accessed=1 << 20) if flops else None
    return pl.pallas_call(
        kernel,
        out_shape=out,
        in_specs=[smem] * scalars + [vmem] * (len(args) - scalars),
        out_specs=jax.tree.map(lambda _: vmem, out),
        cost_estimate=cost,
        scratch_shapes=scratch,
        compiler_params=pltpu.CompilerParams(vmem_limit_bytes=mib << 20),
    )(*args)


CHIP_GROUPS = [[r * 16 + 2 * j + k for r in range(16) for k in range(2)] for j in range(8)]


def exchange_columns(x):
    return lax.all_to_all(
        x, ("row", "col"), split_axis=0, concat_axis=0, axis_index_groups=CHIP_GROUPS, tiled=True
    )


def per_device(signal, norm_gain, qkv_weight, out_weight):
    shape = jax.ShapeDtypeStruct
    r = lax.axis_index("row")
    c = lax.axis_index("col")
    core = lax.rem(c, 2)
    place = jnp.stack([lax.div(c, 8), lax.rem(lax.div(c, 2), 4), lax.div(r, 4), lax.rem(r, 4), core])

    mine = lax.dynamic_slice_in_dim(signal, core * COLS, COLS, 0)
    theirs = core_swap(lax.dynamic_slice_in_dim(signal, (1 - core) * COLS, COLS, 0))
    x = jnp.where(
        core == 0, jnp.concatenate([mine, theirs], axis=1), jnp.concatenate([theirs, mine], axis=1)
    )
    weights = lax.optimization_barrier(jnp.concatenate([qkv_weight, out_weight], axis=1))
    pieces = gather_chips(x)
    weights = over_z_hi(weights)
    own = over_x(weights[..., : 3 * HS])
    other = (core_swap(t) for t in own)
    w = _call(_weights_kernel, shape((2048, 6 * HS), BF16), place, *own, *other, scalars=1)
    moments = _call(
        _early_kernel, (shape((COLS, 1), F32), shape((COLS, 1), F32)), *(pieces[i] for i in EARLY), flops=1 << 30
    )
    qkv = _call(
        _qkv_kernel,
        shape((16, 2, 64, 3 * HS), BF16),
        place,
        norm_gain.reshape(8, 256),
        *moments,
        *pieces,
        w,
        scalars=1,
        scratch=[pltpu.VMEM((TILE, 2048), BF16)] * 2,
    )
    by_column = exchange_columns(qkv.reshape(32, 64, 3 * HS))
    weights, qkv = lax.optimization_barrier((weights[..., 3 * HS :], qkv))
    w = _call(_weights_kernel, shape((2048, HS), BF16), place, *over_x(weights), scalars=1)
    w = jnp.concatenate([w, core_swap(w)], axis=1)
    row = []
    for head in range(2):
        row += _call(
            lambda *refs, head=head: _row_kernel(head, *refs),
            (shape((COLS, HS), F32), shape((64, HS), F32)),
            qkv,
            flops=1 << 33,
        )
    by_column, w, first = lax.optimization_barrier((by_column, w, tuple(row[:2])))
    col_out = _call(_column_kernel, shape((32, 64 + STAT_ROWS, HS), BF16), by_column)
    col_out = exchange_columns(col_out).reshape(16, 2, 64 + STAT_ROWS, HS)
    att = _call(_merge_kernel, shape((COLS, 2 * HS), BF16), *first, *row[2:], col_out)
    out_own, out_other = _call(
        _out_kernel, (shape((2 * COLS, HS), BF16), shape((COLS, HS), BF16)), place, x, *gather_chips(att), w, scalars=1
    )
    return lax.dynamic_update_slice_in_dim(out_own, core_swap(out_other), (1 - core) * COLS, 0)


def solution(mesh):
    return jax.shard_map(
        per_device,
        mesh=mesh,
        in_specs=(P("row", "col"), P(), P("row", "col"), P("row", "col")),
        out_specs=P("row", "col"),
        check_vma=False,
    )
```

```python
import math

import jax
import jax.numpy as jnp
from jax import lax
from jax.experimental import pallas as pl
from jax.experimental.pallas import tpu as pltpu
from jax.sharding import PartitionSpec as P


HS = 128
COLS = 1024
EPSILON = 1e-05
NEGATIVE = -1e30
SCALE2 = math.log2(math.e) / math.sqrt(HS)
TILE = 256
G_COLS = 16
STAT_ROWS = 8

BF16 = jnp.bfloat16
F32 = jnp.float32
NT = (((1,), (1,)), ((), ()))


def _col(z, y, c):
    return (z % 2) * 8 + (y % 4) * 2 + c


def _over_col(x, to):
    pairs = [(_col(z, y, c), to(z, y, c)) for z in range(2) for y in range(4) for c in range(2)]
    return lax.ppermute(x, "col", pairs)


def _over_row(x, to):
    pairs = [(z * 4 + h, to(z, h)) for z in range(4) for h in range(4)]
    return lax.ppermute(x, "row", pairs)


def y_up(x):
    return _over_col(x, lambda z, y, c: _col(z, y + 1, c))


def y_down(x):
    return _over_col(x, lambda z, y, c: _col(z, y + 3, c))


def z_swap(x):
    return _over_col(x, lambda z, y, c: _col(z + 1, y, c))


def core_swap(x):
    return _over_col(x, lambda z, y, c: _col(z, y, 1 - c))


def zh_shift(x, d):
    return _over_row(x, lambda z, h: ((z + d) % 4) * 4 + h)


def x_shift(x, d):
    return _over_row(x, lambda z, h: z * 4 + (h + d) % 4)


def gather_chips(x):
    a = y_up(x)
    b = y_down(x)
    p = z_swap(x)
    left = a[:, :HS]
    fl = y_up(left)
    fr = y_down(b[:, HS:])
    pa = y_up(p)
    pb = y_down(p)
    gl = z_swap(fl)
    gr = z_swap(fr)
    return (x, b, fl, fr, a, p, pb, gl, gr, pa)


def over_z_hi(w):
    return jnp.stack([w] + [zh_shift(w, d) for d in (1, 2, 3)])


def over_x(z):
    return (z, *(x_shift(z, d) for d in (1, 2, 3)))


def _weights_kernel(place, *refs):
    out = refs[-1]
    sides = len(refs) // 4
    width = out.shape[1] // sides
    zl, y, zh, x = place[0], place[1], place[2], place[3]
    for dx in range(4):
        for dz in range(4):
            block = lax.rem(zh + 4 - dz, 4) * 4 + lax.rem(x + 4 - dx, 4)
            chip, half = block // 2, lax.rem(block, 2)
            piece = lax.rem(chip // 4 + zl, 2) * 4 + lax.rem(lax.rem(chip, 4) + 4 - y, 4)
            at = pl.multiple_of(piece * 256 + half * 128, 128)
            for side in range(sides):
                out[pl.ds(at, 128), side * width : (side + 1) * width] = refs[4 * side + dx][dz]


def _chunks(refs):
    return [(ref, k * HS) for ref in refs for k in range(ref.shape[1] // HS)]


def _moments(chunks, rows):
    n = TILE
    total = jnp.zeros((n, HS), F32)
    for ref, k in chunks:
        total += ref[rows, pl.ds(k, HS)].astype(F32)
    mean = jnp.sum(total, axis=1, keepdims=True) * (1.0 / (len(chunks) * HS))
    square = jnp.zeros((n, HS), F32)
    for ref, k in chunks:
        v = ref[rows, pl.ds(k, HS)].astype(F32) - mean
        square += v * v
    return mean, jnp.sum(square, axis=1, keepdims=True)


EARLY = (0, 1, 2, 3, 4, 5)
LATE = (6, 7, 8, 9)
EARLY_WIDTH = 1280
LATE_WIDTH = 768


def _early_kernel(*refs):
    chunks = _chunks(refs[:-1])
    out_ref = refs[-1]

    def step(tile, carry):
        rows = pl.ds(pl.multiple_of(tile * TILE, TILE), TILE)
        out_ref[rows, 0:1], out_ref[rows, 1:2] = _moments(chunks, rows)
        return carry

    lax.fori_loop(0, COLS // TILE, step, 0)


def _qkv_kernel(place, gain_ref, early_ref, *refs):
    pieces, (w_ref, out_ref, even_ref, odd_ref) = refs[:10], refs[10:]
    zl, y, core = place[0], place[1], place[4]
    gains = []
    for i in range(8):
        j = lax.rem(zl + i // 4, 2) * 4 + lax.rem(y + i, 4)
        gains.append(gain_ref[pl.ds(j, 1), :])
    gain = jnp.concatenate(gains, axis=1)
    wide = 2048
    chunks = []
    lane = 0
    for ref in pieces:
        for k in range(ref.shape[1] // HS):
            chunks.append((ref, k * HS, lane))
            lane += HS

    def rows_of(tile):
        return pl.ds(pl.multiple_of(tile * TILE, TILE), TILE)

    late = _chunks([pieces[i] for i in LATE])

    def moments_of(tile):
        return _moments(late, rows_of(tile))

    def together(tile, late_mean, late_square):
        mean = early_ref[rows_of(tile), 0:1]
        apart = late_mean - mean
        square = early_ref[rows_of(tile), 1:2] + late_square
        square += apart * apart * (EARLY_WIDTH * LATE_WIDTH / wide)
        return mean + apart * (LATE_WIDTH / wide), lax.rsqrt(square * (1.0 / wide) + EPSILON)

    def norm(tile, mean, rstd, to_ref):
        for ref, k, at in chunks:
            v = ref[rows_of(tile), pl.ds(k, HS)].astype(F32) - mean
            to_ref[:, pl.ds(at, HS)] = (v * rstd * gain[:, at : at + HS]).astype(BF16)

    def project(tile, from_ref, part):
        lanes = pl.ds(part * HS * 2, HS * 2)
        qkv = jnp.dot(from_ref[...], w_ref[:, lanes], preferred_element_type=F32).astype(BF16)
        blocks = pl.ds(tile * (TILE // 64), TILE // 64)
        for k in range(2):
            n = 2 * part + k
            slot = core if n < 3 else 1 - core
            v = qkv[:, k * HS : (k + 1) * HS].reshape(TILE // 64, 64, HS)
            out_ref[blocks, slot, :, (n % 3) * HS : (n % 3 + 1) * HS] = v

    def both(tile, from_ref, later, to_ref):
        moments = moments_of(later)
        project(tile, from_ref, 0)
        mean, rstd = together(later, *moments)
        project(tile, from_ref, 1)
        norm(later, mean, rstd, to_ref)
        project(tile, from_ref, 2)

    count = COLS // TILE
    norm(0, *together(0, *moments_of(0)), even_ref)

    def step(i, carry):
        both(2 * i, even_ref, 2 * i + 1, odd_ref)
        both(2 * i + 1, odd_ref, jnp.minimum(2 * i + 2, count - 1), even_ref)
        return carry

    lax.fori_loop(0, count // 2, step, 0)


def _out_kernel(place, x_ref, *refs):
    pieces, (w_ref, own_ref, other_ref) = refs[:10], refs[10:]
    core = place[4]

    for tile in range(COLS // TILE):
        at = tile * TILE
        v = jnp.concatenate([ref[pl.ds(at, TILE), :] for ref in pieces], axis=1)
        branch = jnp.dot(v, w_ref[...], preferred_element_type=F32)
        left = x_ref[pl.ds(at, TILE), pl.ds(0, HS)].astype(F32)
        right = x_ref[pl.ds(at, TILE), pl.ds(HS, HS)].astype(F32)
        own = jnp.where(core == 0, left, right) + branch[:, :HS]
        other = jnp.where(core == 0, right, left) + branch[:, HS:]
        own_ref[pl.ds(pl.multiple_of(core * COLS + at, TILE), TILE), :] = own.astype(BF16)
        other_ref[pl.ds(at, TILE), :] = other.astype(BF16)


def _row_kernel(head, qkv_ref, out_ref, lse_ref):
    diagonal = lax.broadcasted_iota(jnp.int32, (TILE, TILE), 0) >= lax.broadcasted_iota(
        jnp.int32, (TILE, TILE), 1
    )
    n = TILE // 64
    lane = lax.broadcasted_iota(jnp.int32, (64, HS), 1)
    packed = jnp.zeros((64, HS), F32)

    def part(lo, hi, k):
        v = qkv_ref[lo * n : hi * n, head, :, k * HS : (k + 1) * HS]
        return v.reshape((hi - lo) * TILE, HS)

    for tile in range(COLS // TILE):
        q = part(tile, tile + 1, 0)
        last = lax.dot_general(q, part(tile, tile + 1, 1), NT, preferred_element_type=F32)
        last = jnp.where(diagonal, last, NEGATIVE)
        top = jnp.max(last, axis=1, keepdims=True)
        if tile:
            before = lax.dot_general(q, part(0, tile, 1), NT, preferred_element_type=F32)
            top = jnp.maximum(top, jnp.max(before, axis=1, keepdims=True))
        w = jnp.exp2((last - top) * SCALE2)
        total = jnp.sum(w, axis=1, keepdims=True)
        acc = jnp.dot(w.astype(BF16), part(tile, tile + 1, 2), preferred_element_type=F32)
        if tile:
            w = jnp.exp2((before - top) * SCALE2)
            total += jnp.sum(w, axis=1, keepdims=True)
            acc += jnp.dot(w.astype(BF16), part(0, tile, 2), preferred_element_type=F32)
        out_ref[tile * TILE : (tile + 1) * TILE, :] = acc / total
        lse = top * SCALE2 + jnp.log2(total)
        for k in range(n):
            here = lane == 2 * (tile * n + k) + head
            packed = jnp.where(here, lse[k * 64 : (k + 1) * 64], packed)
    lse_ref[...] = packed


def _column_kernel(z_ref, out_ref):
    t = 32 * G_COLS
    i = lax.broadcasted_iota(jnp.int32, (t, t), 0)
    j = lax.broadcasted_iota(jnp.int32, (t, t), 1)
    valid = (lax.rem(i, G_COLS) == lax.rem(j, G_COLS)) & (i > j)
    bias = jnp.where(valid, 0.0, NEGATIVE)
    token = lax.broadcasted_iota(jnp.int32, (t, 1), 0)
    lane = lax.broadcasted_iota(jnp.int32, (t, HS), 1) - lax.rem(token, G_COLS)
    dest = lax.broadcasted_iota(jnp.int32, (32 * STAT_ROWS, t), 0)
    source = lax.broadcasted_iota(jnp.int32, (32 * STAT_ROWS, t), 1) // G_COLS
    picks = [(dest == source * STAT_ROWS + m).astype(F32).astype(BF16) for m in range(3)]

    spread = jnp.zeros((t, HS), F32)
    for g in range(64 // G_COLS):
        at = g * G_COLS
        z = z_ref[:, at : at + G_COLS, :].reshape(t, 3 * HS)
        s = lax.dot_general(z[:, :HS], z[:, HS : 2 * HS], NT, preferred_element_type=F32) + bias
        top = jnp.max(s, axis=1, keepdims=True)
        w = jnp.exp2((s - top) * SCALE2)
        total = jnp.sum(w, axis=1, keepdims=True)
        acc = jnp.dot(w.astype(BF16), z[:, 2 * HS :], preferred_element_type=F32)
        out_ref[:, at : at + G_COLS, :] = (acc / total).astype(BF16).reshape(32, G_COLS, HS)
        lse = jnp.where(token >= G_COLS, top * SCALE2 + jnp.log2(total), NEGATIVE)
        spread = jnp.where(lane == at, lse, spread)
    stats = jnp.zeros((32 * STAT_ROWS, HS), F32)
    for pick in picks:
        part = spread.astype(BF16)
        spread = spread - part.astype(F32)
        stats += jnp.dot(pick, part, preferred_element_type=F32)
    out_ref[:, 64 : 64 + STAT_ROWS, :] = stats.astype(BF16).reshape(32, STAT_ROWS, HS)


def _merge_kernel(row0_ref, lse0_ref, row1_ref, lse1_ref, col_ref, out_ref):
    stats = col_ref[:, :, 64:, :].reshape(32 * STAT_ROWS, HS)
    source = lax.broadcasted_iota(jnp.int32, (HS, 32 * STAT_ROWS), 1)
    entry = lax.broadcasted_iota(jnp.int32, (HS, 32 * STAT_ROWS), 0)
    picks = [(source == entry * STAT_ROWS + m).astype(F32).astype(BF16) for m in range(3)]
    parts = [jnp.dot(pick, stats, preferred_element_type=F32) for pick in picks]
    cl = (parts[0] + parts[1] + parts[2]).T[:64]
    rl = lse0_ref[...] + lse1_ref[...]
    top = jnp.maximum(cl, rl)
    rf = jnp.exp2(rl - top)
    cf = jnp.exp2(cl - top)
    share = 1.0 / (rf + cf)
    rf = rf * share
    cf = cf * share
    for block in range(16):
        rows = slice(block * 64, (block + 1) * 64)
        for head, row_ref in enumerate((row0_ref, row1_ref)):
            n = 2 * block + head
            o = rf[:, n : n + 1] * row_ref[rows, :] + cf[:, n : n + 1] * col_ref[block, head, :64, :].astype(F32)
            out_ref[rows, head * HS : (head + 1) * HS] = o.astype(BF16)


def _call(kernel, out, *args, scalars=0, flops=0, scratch=(), mib=24):
    vmem = pl.BlockSpec(memory_space=pltpu.VMEM)
    smem = pl.BlockSpec(memory_space=pltpu.SMEM)
    cost = pl.CostEstimate(flops=flops, transcendentals=0, bytes_accessed=1 << 20) if flops else None
    return pl.pallas_call(
        kernel,
        out_shape=out,
        in_specs=[smem] * scalars + [vmem] * (len(args) - scalars),
        out_specs=jax.tree.map(lambda _: vmem, out),
        cost_estimate=cost,
        scratch_shapes=scratch,
        compiler_params=pltpu.CompilerParams(vmem_limit_bytes=mib << 20),
    )(*args)


CHIP_GROUPS = [[r * 16 + 2 * j + k for r in range(16) for k in range(2)] for j in range(8)]


def exchange_columns(x):
    return lax.all_to_all(
        x, ("row", "col"), split_axis=0, concat_axis=0, axis_index_groups=CHIP_GROUPS, tiled=True
    )


def per_device(signal, norm_gain, qkv_weight, out_weight):
    shape = jax.ShapeDtypeStruct
    r = lax.axis_index("row")
    c = lax.axis_index("col")
    core = lax.rem(c, 2)
    place = jnp.stack([lax.div(c, 8), lax.rem(lax.div(c, 2), 4), lax.div(r, 4), lax.rem(r, 4), core])

    mine = lax.dynamic_slice_in_dim(signal, core * COLS, COLS, 0)
    theirs = core_swap(lax.dynamic_slice_in_dim(signal, (1 - core) * COLS, COLS, 0))
    x = jnp.where(
        core == 0, jnp.concatenate([mine, theirs], axis=1), jnp.concatenate([theirs, mine], axis=1)
    )
    weights = lax.optimization_barrier(jnp.concatenate([qkv_weight, out_weight], axis=1))
    pieces = gather_chips(x)
    weights = over_z_hi(weights)
    own = over_x(weights[..., : 3 * HS])
    other = (core_swap(t) for t in own)
    w = _call(_weights_kernel, shape((2048, 6 * HS), BF16), place, *own, *other, scalars=1)
    moments = _call(_early_kernel, shape((COLS, 2), F32), *(pieces[i] for i in EARLY), flops=1 << 30)
    qkv = _call(
        _qkv_kernel,
        shape((16, 2, 64, 3 * HS), BF16),
        place,
        norm_gain.reshape(8, 256),
        moments,
        *pieces,
        w,
        scalars=1,
        scratch=[pltpu.VMEM((TILE, 2048), BF16)] * 2,
    )
    by_column = exchange_columns(qkv.reshape(32, 64, 3 * HS))
    weights, qkv = lax.optimization_barrier((weights[..., 3 * HS :], qkv))
    w = _call(_weights_kernel, shape((2048, HS), BF16), place, *over_x(weights), scalars=1)
    w = jnp.concatenate([w, core_swap(w)], axis=1)
    row = []
    for head in range(2):
        row += _call(
            lambda *refs, head=head: _row_kernel(head, *refs),
            (shape((COLS, HS), F32), shape((64, HS), F32)),
            qkv,
            flops=1 << 33,
        )
    by_column, w, first = lax.optimization_barrier((by_column, w, tuple(row[:2])))
    col_out = _call(_column_kernel, shape((32, 64 + STAT_ROWS, HS), BF16), by_column)
    col_out = exchange_columns(col_out).reshape(16, 2, 64 + STAT_ROWS, HS)
    att = _call(_merge_kernel, shape((COLS, 2 * HS), BF16), *first, *row[2:], col_out)
    out_own, out_other = _call(
        _out_kernel, (shape((2 * COLS, HS), BF16), shape((COLS, HS), BF16)), place, x, *gather_chips(att), w, scalars=1
    )
    return lax.dynamic_update_slice_in_dim(out_own, core_swap(out_other), (1 - core) * COLS, 0)


def solution(mesh):
    return jax.shard_map(
        per_device,
        mesh=mesh,
        in_specs=(P("row", "col"), P(), P("row", "col"), P("row", "col")),
        out_specs=P("row", "col"),
        check_vma=False,
    )
```

```python
import math

import jax
import jax.numpy as jnp
from jax import lax
from jax.experimental import pallas as pl
from jax.experimental.pallas import tpu as pltpu
from jax.sharding import PartitionSpec as P


HS = 128
COLS = 1024
EPSILON = 1e-05
NEGATIVE = -1e30
SCALE2 = math.log2(math.e) / math.sqrt(HS)
TILE = 256
G_COLS = 16
STAT_ROWS = 8

BF16 = jnp.bfloat16
F32 = jnp.float32
NT = (((1,), (1,)), ((), ()))


def _col(z, y, c):
    return (z % 2) * 8 + (y % 4) * 2 + c


def _over_col(x, to):
    pairs = [(_col(z, y, c), to(z, y, c)) for z in range(2) for y in range(4) for c in range(2)]
    return lax.ppermute(x, "col", pairs)


def _over_row(x, to):
    pairs = [(z * 4 + h, to(z, h)) for z in range(4) for h in range(4)]
    return lax.ppermute(x, "row", pairs)


def y_up(x):
    return _over_col(x, lambda z, y, c: _col(z, y + 1, c))


def y_down(x):
    return _over_col(x, lambda z, y, c: _col(z, y + 3, c))


def z_swap(x):
    return _over_col(x, lambda z, y, c: _col(z + 1, y, c))


def core_swap(x):
    return _over_col(x, lambda z, y, c: _col(z, y, 1 - c))


def zh_shift(x, d):
    return _over_row(x, lambda z, h: ((z + d) % 4) * 4 + h)


def x_shift(x, d):
    return _over_row(x, lambda z, h: z * 4 + (h + d) % 4)


def gather_chips(x):
    a = y_up(x)
    b = y_down(x)
    p = z_swap(x)
    left = a[:, :HS]
    fl = y_up(left)
    fr = y_down(b[:, HS:])
    pa = y_up(p)
    pb = y_down(p)
    gl = z_swap(fl)
    gr = z_swap(fr)
    return (x, b, fl, fr, a, p, pb, gl, gr, pa)


def over_z_hi(w):
    return jnp.stack([w] + [zh_shift(w, d) for d in (1, 2, 3)])


def over_x(z):
    return (z, *(x_shift(z, d) for d in (1, 2, 3)))


def _weights_kernel(place, *refs):
    out = refs[-1]
    sides = len(refs) // 4
    width = out.shape[1] // sides
    zl, y, zh, x = place[0], place[1], place[2], place[3]
    for dx in range(4):
        for dz in range(4):
            block = lax.rem(zh + 4 - dz, 4) * 4 + lax.rem(x + 4 - dx, 4)
            chip, half = block // 2, lax.rem(block, 2)
            piece = lax.rem(chip // 4 + zl, 2) * 4 + lax.rem(lax.rem(chip, 4) + 4 - y, 4)
            at = pl.multiple_of(piece * 256 + half * 128, 128)
            for side in range(sides):
                out[pl.ds(at, 128), side * width : (side + 1) * width] = refs[4 * side + dx][dz]


def _chunks(refs):
    return [(ref, k * HS) for ref in refs for k in range(ref.shape[1] // HS)]


def _moments(chunks, rows):
    n = TILE
    total = jnp.zeros((n, HS), F32)
    for ref, k in chunks:
        total += ref[rows, pl.ds(k, HS)].astype(F32)
    mean = jnp.sum(total, axis=1, keepdims=True) * (1.0 / (len(chunks) * HS))
    square = jnp.zeros((n, HS), F32)
    for ref, k in chunks:
        v = ref[rows, pl.ds(k, HS)].astype(F32) - mean
        square += v * v
    return mean, jnp.sum(square, axis=1, keepdims=True)


EARLY = (0, 1, 2, 3, 4, 5)
LATE = (6, 7, 8, 9)
EARLY_WIDTH = 1280
LATE_WIDTH = 768


def _early_kernel(*refs):
    chunks = _chunks(refs[:-1])
    out_ref = refs[-1]

    def step(tile, carry):
        rows = pl.ds(pl.multiple_of(tile * TILE, TILE), TILE)
        out_ref[rows, 0:1], out_ref[rows, 1:2] = _moments(chunks, rows)
        return carry

    lax.fori_loop(0, COLS // TILE, step, 0)


def _qkv_kernel(place, gain_ref, early_ref, *refs):
    pieces, (w_ref, out_ref, even_ref, odd_ref) = refs[:10], refs[10:]
    zl, y, core = place[0], place[1], place[4]
    gains = []
    for i in range(8):
        j = lax.rem(zl + i // 4, 2) * 4 + lax.rem(y + i, 4)
        gains.append(gain_ref[pl.ds(j, 1), :])
    gain = jnp.concatenate(gains, axis=1)
    wide = 2048
    chunks = []
    lane = 0
    for ref in pieces:
        for k in range(ref.shape[1] // HS):
            chunks.append((ref, k * HS, lane))
            lane += HS

    def rows_of(tile):
        return pl.ds(pl.multiple_of(tile * TILE, TILE), TILE)

    late = _chunks([pieces[i] for i in LATE])

    def moments_of(tile):
        return _moments(late, rows_of(tile))

    def together(tile, late_mean, late_square):
        mean = early_ref[rows_of(tile), 0:1]
        apart = late_mean - mean
        square = early_ref[rows_of(tile), 1:2] + late_square
        square += apart * apart * (EARLY_WIDTH * LATE_WIDTH / wide)
        return mean + apart * (LATE_WIDTH / wide), lax.rsqrt(square * (1.0 / wide) + EPSILON)

    def norm(tile, mean, rstd, to_ref):
        for ref, k, at in chunks:
            v = ref[rows_of(tile), pl.ds(k, HS)].astype(F32) - mean
            to_ref[:, pl.ds(at, HS)] = (v * rstd * gain[:, at : at + HS]).astype(BF16)

    def project(tile, from_ref, part):
        lanes = pl.ds(part * HS * 2, HS * 2)
        qkv = jnp.dot(from_ref[...], w_ref[:, lanes], preferred_element_type=F32).astype(BF16)
        blocks = pl.ds(tile * (TILE // 64), TILE // 64)
        for k in range(2):
            n = 2 * part + k
            slot = core if n < 3 else 1 - core
            v = qkv[:, k * HS : (k + 1) * HS].reshape(TILE // 64, 64, HS)
            out_ref[blocks, slot, :, (n % 3) * HS : (n % 3 + 1) * HS] = v

    def both(tile, from_ref, later, to_ref):
        moments = moments_of(later)
        project(tile, from_ref, 0)
        mean, rstd = together(later, *moments)
        project(tile, from_ref, 1)
        norm(later, mean, rstd, to_ref)
        project(tile, from_ref, 2)

    slots = (even_ref, odd_ref)
    count = COLS // TILE
    norm(0, *together(0, *moments_of(0)), even_ref)
    for tile in range(count - 1):
        both(tile, slots[tile % 2], tile + 1, slots[(tile + 1) % 2])
    for part in range(3):
        project(count - 1, slots[(count - 1) % 2], part)


def _out_kernel(place, x_ref, *refs):
    pieces, (w_ref, own_ref, other_ref) = refs[:10], refs[10:]
    core = place[4]

    for tile in range(COLS // TILE):
        at = tile * TILE
        v = jnp.concatenate([ref[pl.ds(at, TILE), :] for ref in pieces], axis=1)
        branch = jnp.dot(v, w_ref[...], preferred_element_type=F32)
        left = x_ref[pl.ds(at, TILE), pl.ds(0, HS)].astype(F32)
        right = x_ref[pl.ds(at, TILE), pl.ds(HS, HS)].astype(F32)
        own = jnp.where(core == 0, left, right) + branch[:, :HS]
        other = jnp.where(core == 0, right, left) + branch[:, HS:]
        own_ref[pl.ds(pl.multiple_of(core * COLS + at, TILE), TILE), :] = own.astype(BF16)
        other_ref[pl.ds(at, TILE), :] = other.astype(BF16)


def _row_kernel(qkv_ref, out_ref, lse_ref):
    diagonal = lax.broadcasted_iota(jnp.int32, (TILE, TILE), 0) >= lax.broadcasted_iota(
        jnp.int32, (TILE, TILE), 1
    )
    n = TILE // 64
    lane = lax.broadcasted_iota(jnp.int32, (64, HS), 1)

    def attend(head, packed):
        def part(lo, hi, k):
            v = qkv_ref[lo * n : hi * n, head, :, k * HS : (k + 1) * HS]
            return v.reshape((hi - lo) * TILE, HS)

        for tile in range(COLS // TILE):
            q = part(tile, tile + 1, 0)
            last = lax.dot_general(q, part(tile, tile + 1, 1), NT, preferred_element_type=F32)
            last = jnp.where(diagonal, last, NEGATIVE)
            top = jnp.max(last, axis=1, keepdims=True)
            if tile:
                before = lax.dot_general(q, part(0, tile, 1), NT, preferred_element_type=F32)
                top = jnp.maximum(top, jnp.max(before, axis=1, keepdims=True))
            w = jnp.exp2((last - top) * SCALE2)
            total = jnp.sum(w, axis=1, keepdims=True)
            acc = jnp.dot(w.astype(BF16), part(tile, tile + 1, 2), preferred_element_type=F32)
            if tile:
                w = jnp.exp2((before - top) * SCALE2)
                total += jnp.sum(w, axis=1, keepdims=True)
                acc += jnp.dot(w.astype(BF16), part(0, tile, 2), preferred_element_type=F32)
            out_ref[head, tile * TILE : (tile + 1) * TILE, :] = acc / total
            lse = top * SCALE2 + jnp.log2(total)
            for k in range(n):
                here = lane == 2 * (tile * n + k) + head
                packed = jnp.where(here, lse[k * 64 : (k + 1) * 64], packed)
        return packed

    lse_ref[...] = lax.fori_loop(0, 2, attend, jnp.zeros((64, HS), F32))


def _column_kernel(z_ref, out_ref):
    t = 32 * G_COLS
    i = lax.broadcasted_iota(jnp.int32, (t, t), 0)
    j = lax.broadcasted_iota(jnp.int32, (t, t), 1)
    valid = (lax.rem(i, G_COLS) == lax.rem(j, G_COLS)) & (i > j)
    bias = jnp.where(valid, 0.0, NEGATIVE)
    token = lax.broadcasted_iota(jnp.int32, (t, 1), 0)
    lane = lax.broadcasted_iota(jnp.int32, (t, HS), 1) - lax.rem(token, G_COLS)
    dest = lax.broadcasted_iota(jnp.int32, (32 * STAT_ROWS, t), 0)
    source = lax.broadcasted_iota(jnp.int32, (32 * STAT_ROWS, t), 1) // G_COLS
    picks = [(dest == source * STAT_ROWS + m).astype(F32).astype(BF16) for m in range(3)]

    spread = jnp.zeros((t, HS), F32)
    for g in range(64 // G_COLS):
        at = g * G_COLS
        z = z_ref[:, at : at + G_COLS, :].reshape(t, 3 * HS)
        s = lax.dot_general(z[:, :HS], z[:, HS : 2 * HS], NT, preferred_element_type=F32) + bias
        top = jnp.max(s, axis=1, keepdims=True)
        w = jnp.exp2((s - top) * SCALE2)
        total = jnp.sum(w, axis=1, keepdims=True)
        acc = jnp.dot(w.astype(BF16), z[:, 2 * HS :], preferred_element_type=F32)
        out_ref[:, at : at + G_COLS, :] = (acc / total).astype(BF16).reshape(32, G_COLS, HS)
        lse = jnp.where(token >= G_COLS, top * SCALE2 + jnp.log2(total), NEGATIVE)
        spread = jnp.where(lane == at, lse, spread)
    stats = jnp.zeros((32 * STAT_ROWS, HS), F32)
    for pick in picks:
        part = spread.astype(BF16)
        spread = spread - part.astype(F32)
        stats += jnp.dot(pick, part, preferred_element_type=F32)
    out_ref[:, 64 : 64 + STAT_ROWS, :] = stats.astype(BF16).reshape(32, STAT_ROWS, HS)


def _merge_kernel(row_ref, lse_ref, col_ref, out_ref):
    stats = col_ref[:, :, 64:, :].reshape(32 * STAT_ROWS, HS)
    source = lax.broadcasted_iota(jnp.int32, (HS, 32 * STAT_ROWS), 1)
    entry = lax.broadcasted_iota(jnp.int32, (HS, 32 * STAT_ROWS), 0)
    picks = [(source == entry * STAT_ROWS + m).astype(F32).astype(BF16) for m in range(3)]
    parts = [jnp.dot(pick, stats, preferred_element_type=F32) for pick in picks]
    cl = (parts[0] + parts[1] + parts[2]).T[:64]
    rl = lse_ref[...]
    top = jnp.maximum(cl, rl)
    rf = jnp.exp2(rl - top)
    cf = jnp.exp2(cl - top)
    share = 1.0 / (rf + cf)
    rf = rf * share
    cf = cf * share
    for block in range(16):
        rows = slice(block * 64, (block + 1) * 64)
        for head in range(2):
            n = 2 * block + head
            o = rf[:, n : n + 1] * row_ref[head, rows, :] + cf[:, n : n + 1] * col_ref[block, head, :64, :].astype(F32)
            out_ref[rows, head * HS : (head + 1) * HS] = o.astype(BF16)


def _call(kernel, out, *args, scalars=0, flops=0, scratch=(), mib=24):
    vmem = pl.BlockSpec(memory_space=pltpu.VMEM)
    smem = pl.BlockSpec(memory_space=pltpu.SMEM)
    cost = pl.CostEstimate(flops=flops, transcendentals=0, bytes_accessed=1 << 20) if flops else None
    return pl.pallas_call(
        kernel,
        out_shape=out,
        in_specs=[smem] * scalars + [vmem] * (len(args) - scalars),
        out_specs=jax.tree.map(lambda _: vmem, out),
        cost_estimate=cost,
        scratch_shapes=scratch,
        compiler_params=pltpu.CompilerParams(vmem_limit_bytes=mib << 20),
    )(*args)


CHIP_GROUPS = [[r * 16 + 2 * j + k for r in range(16) for k in range(2)] for j in range(8)]


def exchange_columns(x):
    return lax.all_to_all(
        x, ("row", "col"), split_axis=0, concat_axis=0, axis_index_groups=CHIP_GROUPS, tiled=True
    )


def per_device(signal, norm_gain, qkv_weight, out_weight):
    shape = jax.ShapeDtypeStruct
    r = lax.axis_index("row")
    c = lax.axis_index("col")
    core = lax.rem(c, 2)
    place = jnp.stack([lax.div(c, 8), lax.rem(lax.div(c, 2), 4), lax.div(r, 4), lax.rem(r, 4), core])

    mine = lax.dynamic_slice_in_dim(signal, core * COLS, COLS, 0)
    theirs = core_swap(lax.dynamic_slice_in_dim(signal, (1 - core) * COLS, COLS, 0))
    x = jnp.where(
        core == 0, jnp.concatenate([mine, theirs], axis=1), jnp.concatenate([theirs, mine], axis=1)
    )
    weights = lax.optimization_barrier(jnp.concatenate([qkv_weight, out_weight], axis=1))
    pieces = gather_chips(x)
    weights = over_z_hi(weights)
    own = over_x(weights[..., : 3 * HS])
    other = (core_swap(t) for t in own)
    w = _call(_weights_kernel, shape((2048, 6 * HS), BF16), place, *own, *other, scalars=1)
    moments = _call(_early_kernel, shape((COLS, 2), F32), *(pieces[i] for i in EARLY), flops=1 << 30)
    qkv = _call(
        _qkv_kernel,
        shape((16, 2, 64, 3 * HS), BF16),
        place,
        norm_gain.reshape(8, 256),
        moments,
        *pieces,
        w,
        scalars=1,
        scratch=[pltpu.VMEM((TILE, 2048), BF16)] * 2,
    )
    by_column = exchange_columns(qkv.reshape(32, 64, 3 * HS))
    weights, qkv = lax.optimization_barrier((weights[..., 3 * HS :], qkv))
    weights = over_x(weights)
    w = _call(_weights_kernel, shape((2048, HS), BF16), place, *weights, scalars=1, flops=1 << 31)
    swapped = core_swap(w)
    w = jnp.concatenate([w, swapped], axis=1)
    row = _call(_row_kernel, (shape((2, COLS, HS), F32), shape((64, HS), F32)), qkv, flops=1 << 33)
    by_column, w = lax.optimization_barrier((by_column, w))
    col_out = _call(_column_kernel, shape((32, 64 + STAT_ROWS, HS), BF16), by_column)
    col_out = exchange_columns(col_out).reshape(16, 2, 64 + STAT_ROWS, HS)
    att = _call(_merge_kernel, shape((COLS, 2 * HS), BF16), *row, col_out)
    out_own, out_other = _call(
        _out_kernel, (shape((2 * COLS, HS), BF16), shape((COLS, HS), BF16)), place, x, *gather_chips(att), w, scalars=1
    )
    return lax.dynamic_update_slice_in_dim(out_own, core_swap(out_other), (1 - core) * COLS, 0)


def solution(mesh):
    return jax.shard_map(
        per_device,
        mesh=mesh,
        in_specs=(P("row", "col"), P(), P("row", "col"), P("row", "col")),
        out_specs=P("row", "col"),
        check_vma=False,
    )
```

```python
import math

import jax
import jax.numpy as jnp
from jax import lax
from jax.experimental import pallas as pl
from jax.experimental.pallas import tpu as pltpu
from jax.sharding import PartitionSpec as P


HS = 128
COLS = 1024
EPSILON = 1e-05
NEGATIVE = -1e30
SCALE2 = math.log2(math.e) / math.sqrt(HS)
TILE = 256
G_COLS = 16
STAT_ROWS = 8

BF16 = jnp.bfloat16
F32 = jnp.float32
NT = (((1,), (1,)), ((), ()))


def _col(z, y, c):
    return (z % 2) * 8 + (y % 4) * 2 + c


def _over_col(x, to):
    pairs = [(_col(z, y, c), to(z, y, c)) for z in range(2) for y in range(4) for c in range(2)]
    return lax.ppermute(x, "col", pairs)


def _over_row(x, to):
    pairs = [(z * 4 + h, to(z, h)) for z in range(4) for h in range(4)]
    return lax.ppermute(x, "row", pairs)


def y_up(x):
    return _over_col(x, lambda z, y, c: _col(z, y + 1, c))


def y_down(x):
    return _over_col(x, lambda z, y, c: _col(z, y + 3, c))


def z_swap(x):
    return _over_col(x, lambda z, y, c: _col(z + 1, y, c))


def core_swap(x):
    return _over_col(x, lambda z, y, c: _col(z, y, 1 - c))


def zh_shift(x, d):
    return _over_row(x, lambda z, h: ((z + d) % 4) * 4 + h)


def x_shift(x, d):
    return _over_row(x, lambda z, h: z * 4 + (h + d) % 4)


def gather_chips(x, halves=None):
    if halves is None:
        a = (y_up(x),)
        left = a[0][:, :HS]
    else:
        a = (y_up(halves[0]), y_up(halves[1]))
        left = a[0]
    b = y_down(x)
    p = z_swap(x)
    fl = y_up(left)
    fr = y_down(b[:, HS:])
    pa = y_up(p)
    pb = y_down(p)
    gl = z_swap(fl)
    gr = z_swap(fr)
    return (x, b, fl, fr, *a, p, pb, gl, gr, pa)


def over_z_hi(w):
    return jnp.stack([w] + [zh_shift(w, d) for d in (1, 2, 3)])


def over_x(z):
    return (z, *(x_shift(z, d) for d in (1, 2, 3)))


def _weights_kernel(place, *refs):
    out = refs[-1]
    sides = len(refs) // 4
    width = out.shape[1] // sides
    zl, y, zh, x = place[0], place[1], place[2], place[3]
    for dx in range(4):
        for dz in range(4):
            block = lax.rem(zh + 4 - dz, 4) * 4 + lax.rem(x + 4 - dx, 4)
            chip, half = block // 2, lax.rem(block, 2)
            piece = lax.rem(chip // 4 + zl, 2) * 4 + lax.rem(lax.rem(chip, 4) + 4 - y, 4)
            at = pl.multiple_of(piece * 256 + half * 128, 128)
            for side in range(sides):
                out[pl.ds(at, 128), side * width : (side + 1) * width] = refs[4 * side + dx][dz]


def _chunks(refs):
    return [(ref, k * HS) for ref in refs for k in range(ref.shape[1] // HS)]


def _moments(chunks, rows):
    n = TILE
    total = jnp.zeros((n, HS), F32)
    for ref, k in chunks:
        total += ref[rows, pl.ds(k, HS)].astype(F32)
    mean = jnp.sum(total, axis=1, keepdims=True) * (1.0 / (len(chunks) * HS))
    square = jnp.zeros((n, HS), F32)
    for ref, k in chunks:
        v = ref[rows, pl.ds(k, HS)].astype(F32) - mean
        square += v * v
    return mean, jnp.sum(square, axis=1, keepdims=True)


EARLY = (0, 1, 2, 3, 4, 5)
LATE = (6, 7, 8, 9)
EARLY_WIDTH = 1280
LATE_WIDTH = 768


def _early_kernel(*refs):
    chunks = _chunks(refs[:-1])
    out_ref = refs[-1]

    def step(tile, carry):
        rows = pl.ds(pl.multiple_of(tile * TILE, TILE), TILE)
        out_ref[rows, 0:1], out_ref[rows, 1:2] = _moments(chunks, rows)
        return carry

    lax.fori_loop(0, COLS // TILE, step, 0)


def _qkv_kernel(place, gain_ref, early_ref, *refs):
    pieces, (w_ref, out_ref, even_ref, odd_ref) = refs[:10], refs[10:]
    zl, y, core = place[0], place[1], place[4]
    gains = []
    for i in range(8):
        j = lax.rem(zl + i // 4, 2) * 4 + lax.rem(y + i, 4)
        gains.append(gain_ref[pl.ds(j, 1), :])
    gain = jnp.concatenate(gains, axis=1)
    wide = 2048
    chunks = []
    lane = 0
    for ref in pieces:
        for k in range(ref.shape[1] // HS):
            chunks.append((ref, k * HS, lane))
            lane += HS

    def rows_of(tile):
        return pl.ds(pl.multiple_of(tile * TILE, TILE), TILE)

    late = _chunks([pieces[i] for i in LATE])

    def moments_of(tile):
        return _moments(late, rows_of(tile))

    def together(tile, late_mean, late_square):
        mean = early_ref[rows_of(tile), 0:1]
        apart = late_mean - mean
        square = early_ref[rows_of(tile), 1:2] + late_square
        square += apart * apart * (EARLY_WIDTH * LATE_WIDTH / wide)
        return mean + apart * (LATE_WIDTH / wide), lax.rsqrt(square * (1.0 / wide) + EPSILON)

    def norm(tile, mean, rstd, to_ref):
        for ref, k, at in chunks:
            v = ref[rows_of(tile), pl.ds(k, HS)].astype(F32) - mean
            to_ref[:, pl.ds(at, HS)] = (v * rstd * gain[:, at : at + HS]).astype(BF16)

    def project(tile, from_ref, part):
        lanes = pl.ds(part * HS * 2, HS * 2)
        qkv = jnp.dot(from_ref[...], w_ref[:, lanes], preferred_element_type=F32).astype(BF16)
        blocks = pl.ds(tile * (TILE // 64), TILE // 64)
        for k in range(2):
            n = 2 * part + k
            slot = core if n < 3 else 1 - core
            v = qkv[:, k * HS : (k + 1) * HS].reshape(TILE // 64, 64, HS)
            out_ref[blocks, slot, :, (n % 3) * HS : (n % 3 + 1) * HS] = v

    def both(tile, from_ref, later, to_ref):
        moments = moments_of(later)
        project(tile, from_ref, 0)
        mean, rstd = together(later, *moments)
        project(tile, from_ref, 1)
        norm(later, mean, rstd, to_ref)
        project(tile, from_ref, 2)

    slots = (even_ref, odd_ref)
    count = COLS // TILE
    norm(0, *together(0, *moments_of(0)), even_ref)
    for tile in range(count - 1):
        both(tile, slots[tile % 2], tile + 1, slots[(tile + 1) % 2])
    for part in range(3):
        project(count - 1, slots[(count - 1) % 2], part)


def _out_kernel(place, x_ref, *refs):
    pieces, (w_ref, own_ref, other_ref) = refs[:-3], refs[-3:]
    core = place[4]

    for tile in range(COLS // TILE):
        at = tile * TILE
        v = jnp.concatenate([ref[pl.ds(at, TILE), :] for ref in pieces], axis=1)
        branch = jnp.dot(v, w_ref[...], preferred_element_type=F32)
        left = x_ref[pl.ds(at, TILE), pl.ds(0, HS)].astype(F32)
        right = x_ref[pl.ds(at, TILE), pl.ds(HS, HS)].astype(F32)
        own = jnp.where(core == 0, left, right) + branch[:, :HS]
        other = jnp.where(core == 0, right, left) + branch[:, HS:]
        own_ref[pl.ds(pl.multiple_of(core * COLS + at, TILE), TILE), :] = own.astype(BF16)
        other_ref[pl.ds(at, TILE), :] = other.astype(BF16)


def _row_kernel(qkv_ref, out_ref, lse_ref):
    diagonal = lax.broadcasted_iota(jnp.int32, (TILE, TILE), 0) >= lax.broadcasted_iota(
        jnp.int32, (TILE, TILE), 1
    )
    n = TILE // 64
    lane = lax.broadcasted_iota(jnp.int32, (64, HS), 1)

    def attend(head, packed):
        def part(lo, hi, k):
            v = qkv_ref[lo * n : hi * n, head, :, k * HS : (k + 1) * HS]
            return v.reshape((hi - lo) * TILE, HS)

        for tile in range(COLS // TILE):
            q = part(tile, tile + 1, 0)
            last = lax.dot_general(q, part(tile, tile + 1, 1), NT, preferred_element_type=F32)
            last = jnp.where(diagonal, last, NEGATIVE)
            top = jnp.max(last, axis=1, keepdims=True)
            if tile:
                before = lax.dot_general(q, part(0, tile, 1), NT, preferred_element_type=F32)
                top = jnp.maximum(top, jnp.max(before, axis=1, keepdims=True))
            w = jnp.exp2((last - top) * SCALE2)
            total = jnp.sum(w, axis=1, keepdims=True)
            acc = jnp.dot(w.astype(BF16), part(tile, tile + 1, 2), preferred_element_type=F32)
            if tile:
                w = jnp.exp2((before - top) * SCALE2)
                total += jnp.sum(w, axis=1, keepdims=True)
                acc += jnp.dot(w.astype(BF16), part(0, tile, 2), preferred_element_type=F32)
            out_ref[head, tile * TILE : (tile + 1) * TILE, :] = acc / total
            lse = top * SCALE2 + jnp.log2(total)
            for k in range(n):
                here = lane == 2 * (tile * n + k) + head
                packed = jnp.where(here, lse[k * 64 : (k + 1) * 64], packed)
        return packed

    lse_ref[...] = lax.fori_loop(0, 2, attend, jnp.zeros((64, HS), F32))


def _column_kernel(z_ref, out_ref):
    t = 32 * G_COLS
    i = lax.broadcasted_iota(jnp.int32, (t, t), 0)
    j = lax.broadcasted_iota(jnp.int32, (t, t), 1)
    valid = (lax.rem(i, G_COLS) == lax.rem(j, G_COLS)) & (i > j)
    bias = jnp.where(valid, 0.0, NEGATIVE)
    token = lax.broadcasted_iota(jnp.int32, (t, 1), 0)
    lane = lax.broadcasted_iota(jnp.int32, (t, HS), 1) - lax.rem(token, G_COLS)
    dest = lax.broadcasted_iota(jnp.int32, (32 * STAT_ROWS, t), 0)
    source = lax.broadcasted_iota(jnp.int32, (32 * STAT_ROWS, t), 1) // G_COLS
    picks = [(dest == source * STAT_ROWS + m).astype(F32).astype(BF16) for m in range(3)]

    spread = jnp.zeros((t, HS), F32)
    for g in range(64 // G_COLS):
        at = g * G_COLS
        z = z_ref[:, at : at + G_COLS, :].reshape(t, 3 * HS)
        s = lax.dot_general(z[:, :HS], z[:, HS : 2 * HS], NT, preferred_element_type=F32) + bias
        top = jnp.max(s, axis=1, keepdims=True)
        w = jnp.exp2((s - top) * SCALE2)
        total = jnp.sum(w, axis=1, keepdims=True)
        acc = jnp.dot(w.astype(BF16), z[:, 2 * HS :], preferred_element_type=F32)
        out_ref[:, at : at + G_COLS, :] = (acc / total).astype(BF16).reshape(32, G_COLS, HS)
        lse = jnp.where(token >= G_COLS, top * SCALE2 + jnp.log2(total), NEGATIVE)
        spread = jnp.where(lane == at, lse, spread)
    stats = jnp.zeros((32 * STAT_ROWS, HS), F32)
    for pick in picks:
        part = spread.astype(BF16)
        spread = spread - part.astype(F32)
        stats += jnp.dot(pick, part, preferred_element_type=F32)
    out_ref[:, 64 : 64 + STAT_ROWS, :] = stats.astype(BF16).reshape(32, STAT_ROWS, HS)


def _merge_kernel(row_ref, lse_ref, col_ref, out_ref, left_ref, right_ref):
    stats = col_ref[:, :, 64:, :].reshape(32 * STAT_ROWS, HS)
    source = lax.broadcasted_iota(jnp.int32, (HS, 32 * STAT_ROWS), 1)
    entry = lax.broadcasted_iota(jnp.int32, (HS, 32 * STAT_ROWS), 0)
    picks = [(source == entry * STAT_ROWS + m).astype(F32).astype(BF16) for m in range(3)]
    parts = [jnp.dot(pick, stats, preferred_element_type=F32) for pick in picks]
    cl = (parts[0] + parts[1] + parts[2]).T[:64]
    rl = lse_ref[...]
    top = jnp.maximum(cl, rl)
    rf = jnp.exp2(rl - top)
    cf = jnp.exp2(cl - top)
    share = 1.0 / (rf + cf)
    rf = rf * share
    cf = cf * share
    for block in range(16):
        rows = slice(block * 64, (block + 1) * 64)
        for head in range(2):
            n = 2 * block + head
            o = rf[:, n : n + 1] * row_ref[head, rows, :] + cf[:, n : n + 1] * col_ref[block, head, :64, :].astype(F32)
            o = o.astype(BF16)
            out_ref[rows, head * HS : (head + 1) * HS] = o
            (left_ref, right_ref)[head][rows, :] = o


def _call(kernel, out, *args, scalars=0, flops=0, scratch=(), mib=24):
    vmem = pl.BlockSpec(memory_space=pltpu.VMEM)
    smem = pl.BlockSpec(memory_space=pltpu.SMEM)
    cost = pl.CostEstimate(flops=flops, transcendentals=0, bytes_accessed=1 << 20) if flops else None
    return pl.pallas_call(
        kernel,
        out_shape=out,
        in_specs=[smem] * scalars + [vmem] * (len(args) - scalars),
        out_specs=jax.tree.map(lambda _: vmem, out),
        cost_estimate=cost,
        scratch_shapes=scratch,
        compiler_params=pltpu.CompilerParams(vmem_limit_bytes=mib << 20),
    )(*args)


CHIP_GROUPS = [[r * 16 + 2 * j + k for r in range(16) for k in range(2)] for j in range(8)]


def exchange_columns(x):
    return lax.all_to_all(
        x, ("row", "col"), split_axis=0, concat_axis=0, axis_index_groups=CHIP_GROUPS, tiled=True
    )


def per_device(signal, norm_gain, qkv_weight, out_weight):
    shape = jax.ShapeDtypeStruct
    r = lax.axis_index("row")
    c = lax.axis_index("col")
    core = lax.rem(c, 2)
    place = jnp.stack([lax.div(c, 8), lax.rem(lax.div(c, 2), 4), lax.div(r, 4), lax.rem(r, 4), core])

    mine = lax.dynamic_slice_in_dim(signal, core * COLS, COLS, 0)
    theirs = core_swap(lax.dynamic_slice_in_dim(signal, (1 - core) * COLS, COLS, 0))
    x = jnp.where(
        core == 0, jnp.concatenate([mine, theirs], axis=1), jnp.concatenate([theirs, mine], axis=1)
    )
    weights = lax.optimization_barrier(jnp.concatenate([qkv_weight, out_weight], axis=1))
    pieces = gather_chips(x)
    weights = over_z_hi(weights)
    own = over_x(weights[..., : 3 * HS])
    other = (core_swap(t) for t in own)
    w = _call(_weights_kernel, shape((2048, 6 * HS), BF16), place, *own, *other, scalars=1)
    moments = _call(_early_kernel, shape((COLS, 2), F32), *(pieces[i] for i in EARLY), flops=1 << 30)
    qkv = _call(
        _qkv_kernel,
        shape((16, 2, 64, 3 * HS), BF16),
        place,
        norm_gain.reshape(8, 256),
        moments,
        *pieces,
        w,
        scalars=1,
        scratch=[pltpu.VMEM((TILE, 2048), BF16)] * 2,
    )
    by_column = exchange_columns(qkv.reshape(32, 64, 3 * HS))
    weights, qkv = lax.optimization_barrier((weights[..., 3 * HS :], qkv))
    weights = over_x(weights)
    w = _call(_weights_kernel, shape((2048, HS), BF16), place, *weights, scalars=1, flops=1 << 31)
    swapped = core_swap(w)
    w = jnp.concatenate([w, swapped], axis=1)
    row = _call(_row_kernel, (shape((2, COLS, HS), F32), shape((64, HS), F32)), qkv, flops=1 << 33)
    by_column, w = lax.optimization_barrier((by_column, w))
    col_out = _call(_column_kernel, shape((32, 64 + STAT_ROWS, HS), BF16), by_column)
    col_out = exchange_columns(col_out).reshape(16, 2, 64 + STAT_ROWS, HS)
    one = shape((COLS, HS), BF16)
    att, *halves = _call(_merge_kernel, (shape((COLS, 2 * HS), BF16), one, one), *row, col_out)
    out_own, out_other = _call(
        _out_kernel,
        (shape((2 * COLS, HS), BF16), shape((COLS, HS), BF16)),
        place,
        x,
        *gather_chips(att, halves),
        w,
        scalars=1,
    )
    return lax.dynamic_update_slice_in_dim(out_own, core_swap(out_other), (1 - core) * COLS, 0)


def solution(mesh):
    return jax.shard_map(
        per_device,
        mesh=mesh,
        in_specs=(P("row", "col"), P(), P("row", "col"), P("row", "col")),
        out_specs=P("row", "col"),
        check_vma=False,
    )
```
